512 devices in a mesh: gx: 64 (over z, x_hi, core), gy: 8 (over y, x_lo).
Axes of the slice: x: 4 (x_hi: 2, x_lo: 2; x = x_hi * 2 + x_lo), y: 4, z: 16, core: 2. Of those that a mesh axis runs over, the one named last changes fastest.
Arguments:
- iterate: float32 [32, 1536, 1024], P(None, 'gx', 'gy'), may hold values from -6 to 6
- source: float32 [32, 1536, 1024], P(None, 'gx', 'gy'), may hold values from -8 to 8
- conduct: float32 [32, 1536, 1024], P(None, 'gx', 'gy'), may hold values from 0.2 to 5
Outputs:
- updated: float32 [32, 1536, 1024], P(None, 'gx', 'gy')
The draws below stay inside these ranges and needn't reach their ends.
All inputs are finite; a program needn't handle non-finite values.
Results may differ from the reference program's by a relative error of at most 0.000041.
Values sent between devices are 32-bit elements; how exact they have to be, the bound alone decides.
A program may use at most 64 MiB of HBM per device.

```python
import math
import jax
import jax.numpy as jnp

NZ = 32
SWEEPS = 3
COARSE_SWEEPS = 4
COARSEN = 8
NX = 1536
NY = 1024


def shard_levels(stream_key, extent, cuts, low, top_value):
    factor_of = 1.0
    for position, blocks in cuts:
        steps = jax.random.uniform(jax.random.fold_in(jax.random.fold_in(stream_key, 6), position), (blocks,), jnp.float32, low / len(cuts), top_value / len(cuts))
        factor_of = factor_of * jnp.repeat(jnp.exp(steps), extent[position] // blocks).reshape((-1,) + (1,) * (len(extent) - 1 - position))
    return factor_of


def centred(rng, shape, deviation, reach, shards=(), held_as=jnp.bfloat16):
    values = deviation * jax.random.normal(rng, shape, jnp.float32)
    if shards:
        values = values * shard_levels(rng, shape, shards, -0.22, 0.18)
    return jnp.clip(values, -reach, reach).astype(held_as)


def setup_inputs(seed: int = 0) -> dict:
    key_list = jax.random.split(jax.random.key(seed), 4)
    return {
        "iterate": centred(key_list[0], (NZ, NX, NY), 1.0, 6.0, ((1, 64), (2, 8)), jnp.float32),
        "source": centred(key_list[1], (NZ, NX, NY), 1.0, 8.0, ((1, 64), (2, 8)), jnp.float32),
        "conduct": jnp.clip(jnp.exp(math.log(5.0) - 3.218876 * jax.random.uniform(key_list[2], (NZ, NX, NY), jnp.float32) ** shard_levels(key_list[2], (NZ, NX, NY), ((1, 64), (2, 8)), -0.2, 0.2)), 0.2, 5.0),
    }


SHIFT = 0.1
LMIN = 0.3
LMAX = 2.0
OMEGA = 0.8


def neighbours(values):
    return [jnp.roll(values, 1, 0), jnp.roll(values, -1, 0), jnp.roll(values, 1, 1), jnp.roll(values, -1, 1), jnp.roll(values, 1, 2), jnp.roll(values, -1, 2)]


def operate(field, cond, factor):
    summed = jnp.zeros_like(field)
    for near_v, near_c in zip(neighbours(field), neighbours(cond)):
        summed = summed + 0.5 * (cond + near_c) * (field - near_v)
    return SHIFT * field + factor * summed


def diagonal(cond, factor):
    summed = jnp.zeros_like(cond)
    for near_c in neighbours(cond):
        summed = summed + 0.5 * (cond + near_c)
    return SHIFT + factor * summed


def restrict(values):
    depth, width_x, width_y = values.shape
    blocks = values.reshape(depth // COARSEN, COARSEN, width_x // COARSEN, COARSEN, width_y // COARSEN, COARSEN)
    return jnp.mean(blocks, axis=(1, 3, 5))


def prolong(values):
    depth, width_x, width_y = values.shape
    spread = jnp.broadcast_to(values[:, None, :, None, :, None], (depth, COARSEN, width_x, COARSEN, width_y, COARSEN))
    return spread.reshape(depth * COARSEN, width_x * COARSEN, width_y * COARSEN)


def reference(iterate, source, conduct):
    theta = (LMAX + LMIN) / 2.0
    delta = (LMAX - LMIN) / 2.0
    sigma = theta / delta
    rho_now = 1.0 / sigma
    residual = source - operate(iterate, conduct, 1.0)
    diag_fine = diagonal(conduct, 1.0)
    correction = jnp.zeros_like(residual)
    remainder = residual
    direction = residual / (theta * diag_fine)
    for sweep_index in range(SWEEPS):
        image = operate(direction, conduct, 1.0)
        correction = correction + direction
        remainder = remainder - image
        rho_next = 1.0 / (2.0 * sigma - rho_now)
        direction = rho_next * rho_now * direction + (2.0 * rho_next / delta) * remainder / diag_fine
        rho_now = rho_next
    correction = correction + direction
    coarse_rhs = restrict(residual)
    coarse_cond = restrict(conduct)
    diag_coarse = diagonal(coarse_cond, 1.0 / 64.0)
    coarse = OMEGA * coarse_rhs / diag_coarse
    for sweep_index in range(COARSE_SWEEPS - 1):
        coarse = coarse + OMEGA * (coarse_rhs - operate(coarse, coarse_cond, 1.0 / 64.0)) / diag_coarse
    return iterate + correction + prolong(coarse)
```

```python
import functools

import jax
import jax.numpy as jnp
from jax import lax
from jax.experimental import pallas as pl
from jax.experimental.pallas import tpu as pltpu
from jax.sharding import PartitionSpec as P

SWEEPS = 3
COARSE_SWEEPS = 4
COARSEN = 8
SHIFT = 0.1
LMIN = 0.3
LMAX = 2.0
OMEGA = 0.8

MESH = pl.DeviceIdType.MESH
NZ, NX, NY = 32, 24, 128
RIM = 4
ROWS = NX + 2 * RIM
NZC, NXC, NYC = NZ // COARSEN, NX // COARSEN, NY // COARSEN
F32 = jnp.float32
NEIGHBOURS = ((1, 0), (-1, 0), (0, 1), (0, -1), (1, 1), (1, -1), (-1, 1), (-1, -1))


def lanes(x, s):
    return pltpu.roll(x, s % x.shape[1], 1)


def rows(x, s):
    return pltpu.roll(x, s % x.shape[0], 0)


def iota(shape, dim):
    return lax.broadcasted_iota(jnp.int32, shape, dim)


def coefficients():
    theta = (LMAX + LMIN) / 2.0
    delta = (LMAX - LMIN) / 2.0
    sigma = theta / delta
    rho = 1.0 / sigma
    steps = []
    for _ in range(SWEEPS):
        after = 1.0 / (2.0 * sigma - rho)
        steps.append((after * rho, 2.0 * after / delta))
        rho = after
    return theta, steps


def kernel(sizes, v_hbm, s_hbm, c_hbm, o_ref, V, C, S, W, RT, D, U, K, KW, KR, KD, EO, PR, MR, ME, CS, CR, XS, XR,
           own_sem, fs, fr, ks, kr, cs, cr, xs, xr):
    ngx, ngy = sizes
    gx, gy = lax.axis_index("gx"), lax.axis_index("gy")

    def at(d):
        return (lax.rem(gx + d[0] + ngx, ngx), lax.rem(gy + d[1] + ngy, ngy))

    barrier = pltpu.get_barrier_semaphore()
    for d in NEIGHBOURS:
        pl.semaphore_signal(barrier, inc=1, device_id=at(d), device_id_type=MESH)
    loads = []
    for i, (src, dst) in enumerate(((v_hbm, V), (c_hbm, C), (s_hbm, S))):
        loads.append(pltpu.make_async_copy(src, dst.at[:, 0:NX, :], own_sem.at[i]))
        loads[-1].start()

    theta, steps = coefficients()
    lane24 = iota((NX, NY), 1)
    lane32 = iota((ROWS, NY), 1)
    lane8 = iota((8, NY), 1)
    row8 = iota((8, NY), 0)

    for zc in range(NZC):
        a, b = iota((NY, NY), 0), iota((NY, NY), 1)
        MR[zc] = jnp.where(b == zc * 32 + 8 + a // COARSEN, 1.0 / COARSEN**3, 0.0).astype(F32)
        ME[zc] = jnp.where(a == zc * 32 + 8 + b // COARSEN, 1.0, 0.0).astype(F32)

    def three_rows(x):
        out = jnp.zeros((8, NY), F32)
        for j in range(NXC):
            out = jnp.where(row8 == j, jnp.sum(x[8 * j : 8 * j + 8], axis=0, keepdims=True), out)
        return out

    def tile_of(sums):
        out = jnp.zeros((8, NY), F32)
        for zc in range(NZC):
            out = out + jnp.dot(three_rows(sums[zc]), MR[zc], precision=lax.Precision.HIGHEST, preferred_element_type=F32)
        return out

    def extract(f, ref):
        def step(m, accs):
            new = []
            for k in range(4):
                z = 4 * m + k
                turned = pltpu.roll(ref[z, 0:NX], 4 * z, 1)
                window = lax.shift_right_logical((lane24 + (8 - 4 * k + NY)) & (NY - 1), 4) == m
                new.append(jnp.where(window, turned, accs[k]))
            return tuple(new)

        accs = lax.fori_loop(0, 8, step, tuple(jnp.zeros((NX, NY), F32) for _ in range(4)))
        phase = lax.shift_right_logical(lane24, 2)

        def pick(j):
            out = accs[0]
            for k in range(1, 4):
                out = jnp.where(((phase + j) & 3) == k, accs[k], out)
            return out

        K[f, 1, 0:NX] = pick(0)
        K[f, 2, 0:NX] = lanes(pick(3), -4)
        K[f, 4, 0:NX] = lanes(pick(1), 4)
        K[f, 3, 0:NX] = lanes(pick(2), 8)

    for i, ref in enumerate((V, C, S)):
        loads[i].wait()
        extract(i, ref)
    csums = []
    for zc in range(NZC):
        csums.append(lax.fori_loop(1, COARSEN, lambda i, a, zc=zc: a + C[zc * COARSEN + i, 0:NX], C[zc * COARSEN, 0:NX]))
    CS[...] = tile_of(csums)

    pl.semaphore_wait(barrier, len(NEIGHBOURS))

    def send(src, dst, send_sem, recv_sem, d):
        copy = pltpu.make_async_remote_copy(
            src_ref=src, dst_ref=dst, send_sem=send_sem, recv_sem=recv_sem, device_id=at(d), device_id_type=MESH
        )
        copy.start()
        return copy

    low, high = slice(NX, NX + RIM), slice(NX + RIM, ROWS)
    first, last = slice(0, RIM), slice(NX - RIM, NX)
    diag_copies = [
        send(K.at[:, 4, last], K.at[:, 0, high], ks.at[4], kr.at[4], (1, 1)),
        send(K.at[:, 1, last], K.at[:, 5, high], ks.at[5], kr.at[5], (1, -1)),
        send(K.at[:, 4, first], K.at[:, 0, low], ks.at[6], kr.at[6], (-1, 1)),
        send(K.at[:, 1, first], K.at[:, 5, low], ks.at[7], kr.at[7], (-1, -1)),
    ]
    near_copies = []
    for i, (src, dst) in enumerate(((v_hbm, V), (c_hbm, C), (s_hbm, S))):
        near_copies.append(send(src.at[:, last, :], dst.at[:, high, :], fs.at[2 * i], fr.at[2 * i], (1, 0)))
        near_copies.append(send(src.at[:, first, :], dst.at[:, low, :], fs.at[2 * i + 1], fr.at[2 * i + 1], (-1, 0)))
    side_copies = [
        send(K.at[:, 1:5, last], K.at[:, 1:5, high], ks.at[0], kr.at[0], (1, 0)),
        send(K.at[:, 1:5, first], K.at[:, 1:5, low], ks.at[1], kr.at[1], (-1, 0)),
    ]
    strip_copies = [
        send(K.at[:, 4, 0:NX], K.at[:, 0, 0:NX], ks.at[2], kr.at[2], (0, 1)),
        send(K.at[:, 1, 0:NX], K.at[:, 5, 0:NX], ks.at[3], kr.at[3], (0, -1)),
    ]
    cond_copies = [send(CS, CR.at[i], cs.at[i], cr.at[i], d) for i, d in enumerate(NEIGHBOURS)]


    for copy in near_copies:
        copy.wait_recv()
    not_last = lane32 != NY - 1
    not_first = lane32 != 0

    def setup(z, acc):
        up, dn = (z + 1) & (NZ - 1), (z + NZ - 1) & (NZ - 1)
        c, v = C[z], V[z]
        ws = [
            c + C[up],
            c + C[dn],
            c + rows(c, -1),
            c + rows(c, 1),
            jnp.where(not_last, c + lanes(c, -1), 0.0),
            jnp.where(not_first, c + lanes(c, 1), 0.0),
        ]
        vs = [V[up], V[dn], rows(v, -1), rows(v, 1), lanes(v, -1), lanes(v, 1)]
        total = ((ws[0] + ws[1]) + (ws[2] + ws[3])) + (ws[4] + ws[5])
        flow = ((ws[0] * vs[0] + ws[1] * vs[1]) + (ws[2] * vs[2] + ws[3] * vs[3])) + (ws[4] * vs[4] + ws[5] * vs[5])
        diag = SHIFT + 0.5 * total
        residual = (S[z] - diag * v) + 0.5 * flow
        inv = 1.0 / diag
        half = 0.5 * inv
        for i in range(6):
            W[i, z] = ws[i] * half
        rt = residual * inv
        RT[z] = rt
        D[0, z] = rt * (1.0 / theta)
        return acc + residual[0:NX]

    rsums = []
    for zc in range(NZC):
        rsums.append(lax.fori_loop(zc * COARSEN, (zc + 1) * COARSEN, setup, jnp.zeros((NX, NY), F32)))

    for copy in strip_copies + cond_copies[:4]:
        copy.wait_recv()
    col0 = (lane24 & 3) == 0

    def face(outer, inner, turn_outer, turn_inner):
        vo, vi, co, ci = K[0, outer, 0:NX], K[0, inner, 0:NX], K[1, outer, 0:NX], K[1, inner, 0:NX]
        if turn_outer:
            vo, co = lanes(vo, turn_outer), lanes(co, turn_outer)
        if turn_inner:
            vi, ci = lanes(vi, turn_inner), lanes(ci, turn_inner)
        flux = jnp.where(col0, 0.5 * (co + ci) * (vo - vi), 0.0)
        for s in (4, 8, 16):
            flux = flux + lanes(flux, -s)
        return three_rows(flux) * (1.0 / COARSEN**3)

    rhs = tile_of(rsums)
    rhs = rhs + jnp.where((lane8 & 31) == 8, lanes(face(0, 1, -3, 0), 8), 0.0)
    rhs = rhs + jnp.where((lane8 & 31) == 23, lanes(face(5, 4, 0, -3), 23), 0.0)

    spot = lane8 & 31

    def widen(left, centre, right):
        out = jnp.where((spot >= 8) & (spot < 24), centre, 0.0)
        if left is not None:
            out = jnp.where((spot >= 4) & (spot < 8), lanes(left, -16), out)
            out = jnp.where((spot >= 24) & (spot < 28), lanes(right, 16), out)
        return out

    def stack(below, centre, above):
        top = jnp.where(row8 < 3, centre, jnp.where(row8 < 6, rows(above, 3), 0.0))
        bottom = jnp.where(row8 >= 5, rows(below, 5), 0.0)
        return jnp.concatenate([top, bottom], axis=0)

    def coarse_weights(c):
        c = c * (0.5 / COARSEN**2)
        ws = [c + lanes(c, 32), c + lanes(c, -32), c + rows(c, -1), c + rows(c, 1), c + lanes(c, -1), c + lanes(c, 1)]
        diag = SHIFT + (((ws[0] + ws[1]) + (ws[2] + ws[3])) + (ws[4] + ws[5]))
        inv = OMEGA / diag
        return inv, ws

    own = CS[...]
    inv, _ = coarse_weights(stack(CR[0], widen(CR[2], own, CR[3]), CR[1]))
    XS[...] = rhs * inv[0:8]
    start_copies = [send(XS, XR.at[i], xs.at[i], xr.at[i], d) for i, d in enumerate(NEIGHBOURS)]

    def image(z, d):
        up, dn = (z + 1) & (NZ - 1), (z + NZ - 1) & (NZ - 1)
        c = D[d, z]
        near = [D[d, up], D[d, dn], rows(c, -1), rows(c, 1), lanes(c, -1), lanes(c, 1)]
        terms = [W[i, z] * near[i] for i in range(6)]
        return c, ((terms[0] + terms[1]) + (terms[2] + terms[3])) + (terms[4] + terms[5])

    def sweep_one(z, carry):
        c, gain = image(z, 0)
        rt = (RT[z] - c) + gain
        RT[z] = rt
        D[1, z] = steps[0][0] * c + steps[0][1] * rt
        return carry

    def sweep_two(z, carry):
        c, gain = image(z, 1)
        rt = (RT[z] - c) + gain
        RT[z] = rt
        d = steps[1][0] * c + steps[1][1] * rt
        D[2, z] = d
        U[z] = D[0, z, 0:NX] + c[0:NX] + d[0:NX]
        return carry

    lax.fori_loop(0, NZ, sweep_one, 0)
    lax.fori_loop(0, NZ, sweep_two, 0)

    for copy in side_copies + diag_copies:
        copy.wait_recv()
    column = lane32 & 3
    ends, starts = column == 3, column == 0

    def strip_near(ref_of, g):
        x = ref_of(g)
        after, before = lanes(x, -1), lanes(x, 1)
        if g not in (2, 5):
            after = jnp.where(ends, lanes(ref_of(g + 1), 3), after)
        if g not in (0, 3):
            before = jnp.where(starts, lanes(ref_of(g - 1), -3), before)
        return x, [lanes(x, -4), lanes(x, 4), rows(x, -1), rows(x, 1), after, before]

    for g in range(6):
        c, cs_ = strip_near(lambda i: K[1, i], g)
        v, vs = strip_near(lambda i: K[0, i], g)
        ws = [c + n for n in cs_]
        total = ((ws[0] + ws[1]) + (ws[2] + ws[3])) + (ws[4] + ws[5])
        flow = ws[0] * vs[0]
        for i in range(1, 6):
            flow = flow + ws[i] * vs[i]
        diag = SHIFT + 0.5 * total
        inv = 1.0 / diag
        half = 0.5 * inv
        for i in range(6):
            KW[i, g] = ws[i] * half
        rt = ((K[2, g] - diag * v) + 0.5 * flow) * inv
        KR[g] = rt
        KD[0, g] = rt * (1.0 / theta)
    for k in range(SWEEPS):
        for g in range(6) if k < SWEEPS - 1 else (1, 4):
            c, near = strip_near(lambda i: KD[k, i], g)
            rt = KR[g] - c
            for i in range(6):
                rt = rt + KW[i, g] * near[i]
            KR[g] = rt
            KD[k + 1, g] = steps[k][0] * c + steps[k][1] * rt
    left = ((KD[0, 1] + KD[1, 1]) + (KD[2, 1] + KD[3, 1]))[0:NX]
    right = ((KD[0, 4] + KD[1, 4]) + (KD[2, 4] + KD[3, 4]))[0:NX]
    left = lanes(left, 4)
    even = (lane24 & 7) < 4
    EO[0] = jnp.where(even, right, left)
    EO[1] = jnp.where(even, left, right)

    for copy in cond_copies[4:] + start_copies:
        copy.wait_recv()

    def extended(ref, own):
        return stack(
            widen(ref[4], ref[0], ref[5]), widen(ref[2], own, ref[3]), widen(ref[6], ref[1], ref[7])
        )

    inv, ws = coarse_weights(extended(CR, own))
    ws = [w * inv for w in ws]
    start = extended(XR, XS[...])
    x = start
    for _ in range(COARSE_SWEEPS - 1):
        near = [lanes(x, 32), lanes(x, -32), rows(x, -1), rows(x, 1), lanes(x, -1), lanes(x, 1)]
        terms = [ws[i] * near[i] for i in range(6)]
        gain = ((terms[0] + terms[1]) + (terms[2] + terms[3])) + (terms[4] + terms[5])
        x = (start + (1.0 - OMEGA) * x) + gain
    x = x[0:8]
    for zc in range(NZC):
        spread = jnp.dot(x, ME[zc], precision=lax.Precision.HIGHEST, preferred_element_type=F32)
        for j in range(NXC):
            PR[zc, 8 * j : 8 * j + 8] = jnp.broadcast_to(spread[j : j + 1], (8, NY))

    edge = (lane24 < 4) | (lane24 >= NY - 4)

    def finish(z, carry):
        c, gain = image(z, 2)
        rt = (RT[z] - c) + gain
        d = steps[2][0] * c + steps[2][1] * rt
        total = U[z] + d[0:NX]
        strip = pltpu.roll(EO[z & 1], (2 * NY - 4 - 4 * z) & (NY - 1), 1)
        total = jnp.where(edge, strip, total)
        o_ref[z] = (V[z, 0:NX] + total) + PR[z // COARSEN]
        return carry

    lax.fori_loop(0, NZ, finish, 0)
    for copy in near_copies + side_copies + strip_copies + diag_copies + cond_copies + start_copies:
        copy.wait_send()


def solution(mesh):
    sizes = (mesh.shape["gx"], mesh.shape["gy"])

    def body(iterate, source, conduct):
        plane = (NZ, ROWS, NY)
        dma = pltpu.SemaphoreType.DMA
        return pl.pallas_call(
            functools.partial(kernel, sizes),
            out_shape=jax.ShapeDtypeStruct((NZ, NX, NY), F32),
            in_specs=[pl.BlockSpec(memory_space=pl.ANY)] * 3,
            out_specs=pl.BlockSpec(memory_space=pltpu.VMEM),
            scratch_shapes=[
                pltpu.VMEM(plane, F32),
                pltpu.VMEM(plane, F32),
                pltpu.VMEM(plane, F32),
                pltpu.VMEM((6,) + plane, F32),
                pltpu.VMEM(plane, F32),
                pltpu.VMEM((3,) + plane, F32),
                pltpu.VMEM((NZ, NX, NY), F32),
                pltpu.VMEM((3, 6, ROWS, NY), F32),
                pltpu.VMEM((6, 6, ROWS, NY), F32),
                pltpu.VMEM((6, ROWS, NY), F32),
                pltpu.VMEM((4, 6, ROWS, NY), F32),
                pltpu.VMEM((2, NX, NY), F32),
                pltpu.VMEM((NZC, NX, NY), F32),
                pltpu.VMEM((NZC, NY, NY), F32),
                pltpu.VMEM((NZC, NY, NY), F32),
                pltpu.VMEM((8, NY), F32),
                pltpu.VMEM((8, 8, NY), F32),
                pltpu.VMEM((8, NY), F32),
                pltpu.VMEM((8, 8, NY), F32),
                dma((3,)),
                dma((6,)),
                dma((6,)),
                dma((8,)),
                dma((8,)),
                dma((8,)),
                dma((8,)),
                dma((8,)),
                dma((8,)),
            ],
            compiler_params=pltpu.CompilerParams(collective_id=0, has_side_effects=True),
        )(iterate, source, conduct)

    return jax.shard_map(
        body,
        mesh=mesh,
        in_specs=(P(None, "gx", "gy"), P(None, "gx", "gy"), P(None, "gx", "gy")),
        out_specs=P(None, "gx", "gy"),
        check_vma=False,
    )
```

```python
import functools

import jax
import jax.numpy as jnp
from jax import lax
from jax.experimental import pallas as pl
from jax.experimental.pallas import tpu as pltpu
from jax.sharding import PartitionSpec as P

SWEEPS = 3
COARSE_SWEEPS = 4
COARSEN = 8
SHIFT = 0.1
LMIN = 0.3
LMAX = 2.0
OMEGA = 0.8

MESH = pl.DeviceIdType.MESH
NZ, NX, NY = 32, 24, 128
RIM = 4
ROWS = NX + 2 * RIM
NZC, NXC, NYC = NZ // COARSEN, NX // COARSEN, NY // COARSEN
UNROLL = 8
F32 = jnp.float32
NEIGHBOURS = ((1, 0), (-1, 0), (0, 1), (0, -1), (1, 1), (1, -1), (-1, 1), (-1, -1))


def lanes(x, s):
    return pltpu.roll(x, s % x.shape[1], 1)


def rows(x, s):
    return pltpu.roll(x, s % x.shape[0], 0)


def iota(shape, dim):
    return lax.broadcasted_iota(jnp.int32, shape, dim)


def coefficients():
    theta = (LMAX + LMIN) / 2.0
    delta = (LMAX - LMIN) / 2.0
    sigma = theta / delta
    rho = 1.0 / sigma
    steps = []
    for _ in range(SWEEPS):
        after = 1.0 / (2.0 * sigma - rho)
        steps.append((after * rho, 2.0 * after / delta))
        rho = after
    return theta, steps


def kernel(sizes, v_hbm, s_hbm, c_hbm, o_ref, V, C, S, W, RT, D, U, K, KW, KR, KD, EO, PR, MR, ME, CS, CR, XS, XR,
           own_sem, fs, fr, ks, kr, cs, cr, xs, xr):
    ngx, ngy = sizes
    gx, gy = lax.axis_index("gx"), lax.axis_index("gy")

    def at(d):
        return (lax.rem(gx + d[0] + ngx, ngx), lax.rem(gy + d[1] + ngy, ngy))

    barrier = pltpu.get_barrier_semaphore()
    for d in NEIGHBOURS:
        pl.semaphore_signal(barrier, inc=1, device_id=at(d), device_id_type=MESH)
    loads = []
    for i, (src, dst) in enumerate(((v_hbm, V), (c_hbm, C), (s_hbm, S))):
        loads.append(pltpu.make_async_copy(src, dst.at[:, 0:NX, :], own_sem.at[i]))
        loads[-1].start()

    theta, steps = coefficients()
    lane24 = iota((NX, NY), 1)
    lane32 = iota((ROWS, NY), 1)
    lane8 = iota((8, NY), 1)
    row8 = iota((8, NY), 0)

    for zc in range(NZC):
        a, b = iota((NY, NY), 0), iota((NY, NY), 1)
        MR[zc] = jnp.where(b == zc * 32 + 8 + a // COARSEN, 1.0 / COARSEN**3, 0.0).astype(F32)
        ME[zc] = jnp.where(a == zc * 32 + 8 + b // COARSEN, 1.0, 0.0).astype(F32)

    def three_rows(x):
        out = jnp.zeros((8, NY), F32)
        for j in range(NXC):
            out = jnp.where(row8 == j, jnp.sum(x[8 * j : 8 * j + 8], axis=0, keepdims=True), out)
        return out

    def tile_of(sums):
        out = jnp.zeros((8, NY), F32)
        for zc in range(NZC):
            out = out + jnp.dot(three_rows(sums[zc]), MR[zc], precision=lax.Precision.HIGHEST, preferred_element_type=F32)
        return out

    def extract(f, ref):
        def step(m, accs):
            new = []
            for k in range(4):
                z = 4 * m + k
                turned = pltpu.roll(ref[z, 0:NX], 4 * z, 1)
                window = lax.shift_right_logical((lane24 + (8 - 4 * k + NY)) & (NY - 1), 4) == m
                new.append(jnp.where(window, turned, accs[k]))
            return tuple(new)

        accs = lax.fori_loop(0, 8, step, tuple(jnp.zeros((NX, NY), F32) for _ in range(4)), unroll=True)
        phase = lax.shift_right_logical(lane24, 2)

        def pick(j):
            out = accs[0]
            for k in range(1, 4):
                out = jnp.where(((phase + j) & 3) == k, accs[k], out)
            return out

        K[f, 1, 0:NX] = pick(0)
        K[f, 2, 0:NX] = lanes(pick(3), -4)
        K[f, 4, 0:NX] = lanes(pick(1), 4)
        K[f, 3, 0:NX] = lanes(pick(2), 8)

    for i, ref in enumerate((V, C, S)):
        loads[i].wait()
        extract(i, ref)
    csums = []
    for zc in range(NZC):
        csums.append(functools.reduce(jnp.add, [C[zc * COARSEN + i, 0:NX] for i in range(COARSEN)]))
    CS[...] = tile_of(csums)

    pl.semaphore_wait(barrier, len(NEIGHBOURS))

    def send(src, dst, send_sem, recv_sem, d):
        copy = pltpu.make_async_remote_copy(
            src_ref=src, dst_ref=dst, send_sem=send_sem, recv_sem=recv_sem, device_id=at(d), device_id_type=MESH
        )
        copy.start()
        return copy

    low, high = slice(NX, NX + RIM), slice(NX + RIM, ROWS)
    first, last = slice(0, RIM), slice(NX - RIM, NX)
    diag_copies = [
        send(K.at[:, 4, last], K.at[:, 0, high], ks.at[4], kr.at[4], (1, 1)),
        send(K.at[:, 1, last], K.at[:, 5, high], ks.at[5], kr.at[5], (1, -1)),
        send(K.at[:, 4, first], K.at[:, 0, low], ks.at[6], kr.at[6], (-1, 1)),
        send(K.at[:, 1, first], K.at[:, 5, low], ks.at[7], kr.at[7], (-1, -1)),
    ]
    near_copies = []
    for i, (src, dst) in enumerate(((v_hbm, V), (c_hbm, C), (s_hbm, S))):
        near_copies.append(send(src.at[:, last, :], dst.at[:, high, :], fs.at[2 * i], fr.at[2 * i], (1, 0)))
        near_copies.append(send(src.at[:, first, :], dst.at[:, low, :], fs.at[2 * i + 1], fr.at[2 * i + 1], (-1, 0)))
    side_copies = [
        send(K.at[:, 1:5, last], K.at[:, 1:5, high], ks.at[0], kr.at[0], (1, 0)),
        send(K.at[:, 1:5, first], K.at[:, 1:5, low], ks.at[1], kr.at[1], (-1, 0)),
    ]
    strip_copies = [
        send(K.at[:, 4, 0:NX], K.at[:, 0, 0:NX], ks.at[2], kr.at[2], (0, 1)),
        send(K.at[:, 1, 0:NX], K.at[:, 5, 0:NX], ks.at[3], kr.at[3], (0, -1)),
    ]
    cond_copies = [send(CS, CR.at[i], cs.at[i], cr.at[i], d) for i, d in enumerate(NEIGHBOURS)]


    for copy in near_copies:
        copy.wait_recv()
    not_last = lane32 != NY - 1
    not_first = lane32 != 0

    def setup(z, acc):
        up, dn = (z + 1) & (NZ - 1), (z + NZ - 1) & (NZ - 1)
        c, v = C[z], V[z]
        ws = [
            c + C[up],
            c + C[dn],
            c + rows(c, -1),
            c + rows(c, 1),
            jnp.where(not_last, c + lanes(c, -1), 0.0),
            jnp.where(not_first, c + lanes(c, 1), 0.0),
        ]
        vs = [V[up], V[dn], rows(v, -1), rows(v, 1), lanes(v, -1), lanes(v, 1)]
        total = ((ws[0] + ws[1]) + (ws[2] + ws[3])) + (ws[4] + ws[5])
        flow = ((ws[0] * vs[0] + ws[1] * vs[1]) + (ws[2] * vs[2] + ws[3] * vs[3])) + (ws[4] * vs[4] + ws[5] * vs[5])
        diag = SHIFT + 0.5 * total
        residual = (S[z] - diag * v) + 0.5 * flow
        inv = 1.0 / diag
        half = 0.5 * inv
        for i in range(6):
            W[i, z] = ws[i] * half
        rt = residual * inv
        RT[z] = rt
        D[0, z] = rt * (1.0 / theta)
        return acc + residual[0:NX]

    rsums = []
    for zc in range(NZC):
        rsums.append(lax.fori_loop(zc * COARSEN, (zc + 1) * COARSEN, setup, jnp.zeros((NX, NY), F32), unroll=True))

    for copy in strip_copies + cond_copies[:4]:
        copy.wait_recv()
    col0 = (lane24 & 3) == 0

    def face(outer, inner, turn_outer, turn_inner):
        vo, vi, co, ci = K[0, outer, 0:NX], K[0, inner, 0:NX], K[1, outer, 0:NX], K[1, inner, 0:NX]
        if turn_outer:
            vo, co = lanes(vo, turn_outer), lanes(co, turn_outer)
        if turn_inner:
            vi, ci = lanes(vi, turn_inner), lanes(ci, turn_inner)
        flux = jnp.where(col0, 0.5 * (co + ci) * (vo - vi), 0.0)
        for s in (4, 8, 16):
            flux = flux + lanes(flux, -s)
        return three_rows(flux) * (1.0 / COARSEN**3)

    rhs = tile_of(rsums)
    rhs = rhs + jnp.where((lane8 & 31) == 8, lanes(face(0, 1, -3, 0), 8), 0.0)
    rhs = rhs + jnp.where((lane8 & 31) == 23, lanes(face(5, 4, 0, -3), 23), 0.0)

    spot = lane8 & 31

    def widen(left, centre, right):
        out = jnp.where((spot >= 8) & (spot < 24), centre, 0.0)
        if left is not None:
            out = jnp.where((spot >= 4) & (spot < 8), lanes(left, -16), out)
            out = jnp.where((spot >= 24) & (spot < 28), lanes(right, 16), out)
        return out

    def stack(below, centre, above):
        top = jnp.where(row8 < 3, centre, jnp.where(row8 < 6, rows(above, 3), 0.0))
        bottom = jnp.where(row8 >= 5, rows(below, 5), 0.0)
        return jnp.concatenate([top, bottom], axis=0)

    def coarse_weights(c):
        c = c * (0.5 / COARSEN**2)
        ws = [c + lanes(c, 32), c + lanes(c, -32), c + rows(c, -1), c + rows(c, 1), c + lanes(c, -1), c + lanes(c, 1)]
        diag = SHIFT + (((ws[0] + ws[1]) + (ws[2] + ws[3])) + (ws[4] + ws[5]))
        inv = OMEGA / diag
        return inv, ws

    own = CS[...]
    inv, _ = coarse_weights(stack(CR[0], widen(CR[2], own, CR[3]), CR[1]))
    XS[...] = rhs * inv[0:8]
    start_copies = [send(XS, XR.at[i], xs.at[i], xr.at[i], d) for i, d in enumerate(NEIGHBOURS)]

    def image(z, d):
        up, dn = (z + 1) & (NZ - 1), (z + NZ - 1) & (NZ - 1)
        c = D[d, z]
        near = [D[d, up], D[d, dn], rows(c, -1), rows(c, 1), lanes(c, -1), lanes(c, 1)]
        terms = [W[i, z] * near[i] for i in range(6)]
        return c, ((terms[0] + terms[1]) + (terms[2] + terms[3])) + (terms[4] + terms[5])

    def sweep_one(z, carry):
        c, gain = image(z, 0)
        rt = (RT[z] - c) + gain
        RT[z] = rt
        D[1, z] = steps[0][0] * c + steps[0][1] * rt
        return carry

    def sweep_two(z, carry):
        c, gain = image(z, 1)
        rt = (RT[z] - c) + gain
        RT[z] = rt
        d = steps[1][0] * c + steps[1][1] * rt
        D[2, z] = d
        U[z] = D[0, z, 0:NX] + c[0:NX] + d[0:NX]
        return carry

    lax.fori_loop(0, NZ, sweep_one, 0, unroll=UNROLL)
    lax.fori_loop(0, NZ, sweep_two, 0, unroll=UNROLL)

    for copy in side_copies + diag_copies:
        copy.wait_recv()
    column = lane32 & 3
    ends, starts = column == 3, column == 0

    def strip_near(ref_of, g):
        x = ref_of(g)
        after, before = lanes(x, -1), lanes(x, 1)
        if g not in (2, 5):
            after = jnp.where(ends, lanes(ref_of(g + 1), 3), after)
        if g not in (0, 3):
            before = jnp.where(starts, lanes(ref_of(g - 1), -3), before)
        return x, [lanes(x, -4), lanes(x, 4), rows(x, -1), rows(x, 1), after, before]

    for g in range(6):
        c, cs_ = strip_near(lambda i: K[1, i], g)
        v, vs = strip_near(lambda i: K[0, i], g)
        ws = [c + n for n in cs_]
        total = ((ws[0] + ws[1]) + (ws[2] + ws[3])) + (ws[4] + ws[5])
        flow = ws[0] * vs[0]
        for i in range(1, 6):
            flow = flow + ws[i] * vs[i]
        diag = SHIFT + 0.5 * total
        inv = 1.0 / diag
        half = 0.5 * inv
        for i in range(6):
            KW[i, g] = ws[i] * half
        rt = ((K[2, g] - diag * v) + 0.5 * flow) * inv
        KR[g] = rt
        KD[0, g] = rt * (1.0 / theta)
    for k in range(SWEEPS):
        for g in range(6) if k < SWEEPS - 1 else (1, 4):
            c, near = strip_near(lambda i: KD[k, i], g)
            rt = KR[g] - c
            for i in range(6):
                rt = rt + KW[i, g] * near[i]
            KR[g] = rt
            KD[k + 1, g] = steps[k][0] * c + steps[k][1] * rt
    left = ((KD[0, 1] + KD[1, 1]) + (KD[2, 1] + KD[3, 1]))[0:NX]
    right = ((KD[0, 4] + KD[1, 4]) + (KD[2, 4] + KD[3, 4]))[0:NX]
    left = lanes(left, 4)
    even = (lane24 & 7) < 4
    EO[0] = jnp.where(even, right, left)
    EO[1] = jnp.where(even, left, right)

    for copy in cond_copies[4:] + start_copies:
        copy.wait_recv()

    def extended(ref, own):
        return stack(
            widen(ref[4], ref[0], ref[5]), widen(ref[2], own, ref[3]), widen(ref[6], ref[1], ref[7])
        )

    inv, ws = coarse_weights(extended(CR, own))
    ws = [w * inv for w in ws]
    start = extended(XR, XS[...])
    x = start
    for _ in range(COARSE_SWEEPS - 1):
        near = [lanes(x, 32), lanes(x, -32), rows(x, -1), rows(x, 1), lanes(x, -1), lanes(x, 1)]
        terms = [ws[i] * near[i] for i in range(6)]
        gain = ((terms[0] + terms[1]) + (terms[2] + terms[3])) + (terms[4] + terms[5])
        x = (start + (1.0 - OMEGA) * x) + gain
    x = x[0:8]
    for zc in range(NZC):
        spread = jnp.dot(x, ME[zc], precision=lax.Precision.HIGHEST, preferred_element_type=F32)
        for j in range(NXC):
            PR[zc, 8 * j : 8 * j + 8] = jnp.broadcast_to(spread[j : j + 1], (8, NY))

    edge = (lane24 < 4) | (lane24 >= NY - 4)

    def finish(z, carry):
        c, gain = image(z, 2)
        rt = (RT[z] - c) + gain
        d = steps[2][0] * c + steps[2][1] * rt
        total = U[z] + d[0:NX]
        strip = pltpu.roll(EO[z & 1], (2 * NY - 4 - 4 * z) & (NY - 1), 1)
        total = jnp.where(edge, strip, total)
        o_ref[z] = (V[z, 0:NX] + total) + PR[z // COARSEN]
        return carry

    lax.fori_loop(0, NZ, finish, 0, unroll=UNROLL)
    for copy in near_copies + side_copies + strip_copies + diag_copies + cond_copies + start_copies:
        copy.wait_send()


def solution(mesh):
    sizes = (mesh.shape["gx"], mesh.shape["gy"])

    def body(iterate, source, conduct):
        plane = (NZ, ROWS, NY)
        dma = pltpu.SemaphoreType.DMA
        return pl.pallas_call(
            functools.partial(kernel, sizes),
            out_shape=jax.ShapeDtypeStruct((NZ, NX, NY), F32),
            in_specs=[pl.BlockSpec(memory_space=pl.ANY)] * 3,
            out_specs=pl.BlockSpec(memory_space=pltpu.VMEM),
            scratch_shapes=[
                pltpu.VMEM(plane, F32),
                pltpu.VMEM(plane, F32),
                pltpu.VMEM(plane, F32),
                pltpu.VMEM((6,) + plane, F32),
                pltpu.VMEM(plane, F32),
                pltpu.VMEM((3,) + plane, F32),
                pltpu.VMEM((NZ, NX, NY), F32),
                pltpu.VMEM((3, 6, ROWS, NY), F32),
                pltpu.VMEM((6, 6, ROWS, NY), F32),
                pltpu.VMEM((6, ROWS, NY), F32),
                pltpu.VMEM((4, 6, ROWS, NY), F32),
                pltpu.VMEM((2, NX, NY), F32),
                pltpu.VMEM((NZC, NX, NY), F32),
                pltpu.VMEM((NZC, NY, NY), F32),
                pltpu.VMEM((NZC, NY, NY), F32),
                pltpu.VMEM((8, NY), F32),
                pltpu.VMEM((8, 8, NY), F32),
                pltpu.VMEM((8, NY), F32),
                pltpu.VMEM((8, 8, NY), F32),
                dma((3,)),
                dma((6,)),
                dma((6,)),
                dma((8,)),
                dma((8,)),
                dma((8,)),
                dma((8,)),
                dma((8,)),
                dma((8,)),
            ],
            compiler_params=pltpu.CompilerParams(collective_id=0, has_side_effects=True),
        )(iterate, source, conduct)

    return jax.shard_map(
        body,
        mesh=mesh,
        in_specs=(P(None, "gx", "gy"), P(None, "gx", "gy"), P(None, "gx", "gy")),
        out_specs=P(None, "gx", "gy"),
        check_vma=False,
    )
```

```python
import functools

import jax
import jax.numpy as jnp
from jax import lax
from jax.experimental import pallas as pl
from jax.experimental.pallas import tpu as pltpu
from jax.sharding import PartitionSpec as P

SWEEPS = 3
COARSE_SWEEPS = 4
COARSEN = 8
SHIFT = 0.1
LMIN = 0.3
LMAX = 2.0
OMEGA = 0.8

MESH = pl.DeviceIdType.MESH
NZ, NX, NY = 32, 24, 128
RIM = 4
ROWS = NX + 2 * RIM
NZC, NXC, NYC = NZ // COARSEN, NX // COARSEN, NY // COARSEN
UNROLL = 8
F32 = jnp.float32
NEIGHBOURS = ((1, 0), (-1, 0), (0, 1), (0, -1), (1, 1), (1, -1), (-1, 1), (-1, -1))


def lanes(x, s):
    return pltpu.roll(x, s % x.shape[1], 1)


def rows(x, s):
    return pltpu.roll(x, s % x.shape[0], 0)


def iota(shape, dim):
    return lax.broadcasted_iota(jnp.int32, shape, dim)


def coefficients():
    theta = (LMAX + LMIN) / 2.0
    delta = (LMAX - LMIN) / 2.0
    sigma = theta / delta
    rho = 1.0 / sigma
    steps = []
    for _ in range(SWEEPS):
        after = 1.0 / (2.0 * sigma - rho)
        steps.append((after * rho, 2.0 * after / delta))
        rho = after
    return theta, steps


def kernel(sizes, v_hbm, s_hbm, c_hbm, o_ref, V, C, S, W, RT, D, U, K, KW, KR, KD, EO, PR, MR, ME, CS, CR, XS, XR,
           own_sem, fs, fr, ks, kr, cs, cr, xs, xr):
    ngx, ngy = sizes
    gx, gy = lax.axis_index("gx"), lax.axis_index("gy")

    def at(d):
        return (lax.rem(gx + d[0] + ngx, ngx), lax.rem(gy + d[1] + ngy, ngy))

    barrier = pltpu.get_barrier_semaphore()
    for d in NEIGHBOURS:
        pl.semaphore_signal(barrier, inc=1, device_id=at(d), device_id_type=MESH)
    loads = []
    for i, (src, dst) in enumerate(((v_hbm, V), (c_hbm, C), (s_hbm, S))):
        loads.append(pltpu.make_async_copy(src, dst.at[:, 0:NX, :], own_sem.at[i]))
        loads[-1].start()

    theta, steps = coefficients()
    lane24 = iota((NX, NY), 1)
    lane32 = iota((ROWS, NY), 1)
    lane8 = iota((8, NY), 1)
    row8 = iota((8, NY), 0)

    for zc in range(NZC):
        a, b = iota((NY, NY), 0), iota((NY, NY), 1)
        MR[zc] = jnp.where(b == zc * 32 + 8 + a // COARSEN, 1.0 / COARSEN**3, 0.0).astype(F32)
        ME[zc] = jnp.where(a == zc * 32 + 8 + b // COARSEN, 1.0, 0.0).astype(F32)

    def three_rows(x):
        out = jnp.zeros((8, NY), F32)
        for j in range(NXC):
            out = jnp.where(row8 == j, jnp.sum(x[8 * j : 8 * j + 8], axis=0, keepdims=True), out)
        return out

    def tile_of(sums):
        out = jnp.zeros((8, NY), F32)
        for zc in range(NZC):
            out = out + jnp.dot(three_rows(sums[zc]), MR[zc], precision=lax.Precision.HIGHEST, preferred_element_type=F32)
        return out

    def extract(f, ref):
        def step(m, accs):
            new = []
            for k in range(4):
                z = 4 * m + k
                turned = pltpu.roll(ref[z, 0:NX], 4 * z, 1)
                window = lax.shift_right_logical((lane24 + (8 - 4 * k + NY)) & (NY - 1), 4) == m
                new.append(jnp.where(window, turned, accs[k]))
            return tuple(new)

        accs = lax.fori_loop(0, 8, step, tuple(jnp.zeros((NX, NY), F32) for _ in range(4)), unroll=True)
        phase = lax.shift_right_logical(lane24, 2)

        def pick(j):
            out = accs[0]
            for k in range(1, 4):
                out = jnp.where(((phase + j) & 3) == k, accs[k], out)
            return out

        K[f, 1, 0:NX] = pick(0)
        K[f, 2, 0:NX] = lanes(pick(3), -4)
        K[f, 4, 0:NX] = lanes(pick(1), 4)
        K[f, 3, 0:NX] = lanes(pick(2), 8)

    for i, ref in enumerate((V, C, S)):
        loads[i].wait()
        extract(i, ref)
    csums = []
    for zc in range(NZC):
        csums.append(functools.reduce(jnp.add, [C[zc * COARSEN + i, 0:NX] for i in range(COARSEN)]))
    CS[...] = tile_of(csums)

    pl.semaphore_wait(barrier, len(NEIGHBOURS))

    def send(src, dst, send_sem, recv_sem, d):
        copy = pltpu.make_async_remote_copy(
            src_ref=src, dst_ref=dst, send_sem=send_sem, recv_sem=recv_sem, device_id=at(d), device_id_type=MESH
        )
        copy.start()
        return copy

    low, high = slice(NX, NX + RIM), slice(NX + RIM, ROWS)
    first, last = slice(0, RIM), slice(NX - RIM, NX)
    diag_copies = [
        send(K.at[:, 4, last], K.at[:, 0, high], ks.at[4], kr.at[4], (1, 1)),
        send(K.at[:, 1, last], K.at[:, 5, high], ks.at[5], kr.at[5], (1, -1)),
        send(K.at[:, 4, first], K.at[:, 0, low], ks.at[6], kr.at[6], (-1, 1)),
        send(K.at[:, 1, first], K.at[:, 5, low], ks.at[7], kr.at[7], (-1, -1)),
    ]
    near_copies = []
    for i, (src, dst) in enumerate(((v_hbm, V), (c_hbm, C), (s_hbm, S))):
        near_copies.append(send(src.at[:, last, :], dst.at[:, high, :], fs.at[2 * i], fr.at[2 * i], (1, 0)))
        near_copies.append(send(src.at[:, first, :], dst.at[:, low, :], fs.at[2 * i + 1], fr.at[2 * i + 1], (-1, 0)))
    side_copies = [
        send(K.at[:, 1:5, last], K.at[:, 1:5, high], ks.at[0], kr.at[0], (1, 0)),
        send(K.at[:, 1:5, first], K.at[:, 1:5, low], ks.at[1], kr.at[1], (-1, 0)),
    ]
    strip_copies = [
        send(K.at[:, 4, 0:NX], K.at[:, 0, 0:NX], ks.at[2], kr.at[2], (0, 1)),
        send(K.at[:, 1, 0:NX], K.at[:, 5, 0:NX], ks.at[3], kr.at[3], (0, -1)),
    ]
    cond_copies = [send(CS, CR.at[i], cs.at[i], cr.at[i], d) for i, d in enumerate(NEIGHBOURS)]


    for copy in near_copies:
        copy.wait_recv()
    not_last = lane32 != NY - 1
    not_first = lane32 != 0

    def setup(z, acc):
        up, dn = (z + 1) & (NZ - 1), (z + NZ - 1) & (NZ - 1)
        c, v = C[z], V[z]
        ws = [
            c + C[up],
            c + C[dn],
            c + rows(c, -1),
            c + rows(c, 1),
            jnp.where(not_last, c + lanes(c, -1), 0.0),
            jnp.where(not_first, c + lanes(c, 1), 0.0),
        ]
        vs = [V[up], V[dn], rows(v, -1), rows(v, 1), lanes(v, -1), lanes(v, 1)]
        total = ((ws[0] + ws[1]) + (ws[2] + ws[3])) + (ws[4] + ws[5])
        flow = ((ws[0] * vs[0] + ws[1] * vs[1]) + (ws[2] * vs[2] + ws[3] * vs[3])) + (ws[4] * vs[4] + ws[5] * vs[5])
        diag = SHIFT + 0.5 * total
        residual = (S[z] - diag * v) + 0.5 * flow
        inv = 1.0 / diag
        half = 0.5 * inv
        for i in range(6):
            W[i, z] = ws[i] * half
        rt = residual * inv
        RT[z] = rt
        D[0, z] = rt * (1.0 / theta)
        return acc + residual[0:NX]

    rsums = []
    for zc in range(NZC):
        rsums.append(lax.fori_loop(zc * COARSEN, (zc + 1) * COARSEN, setup, jnp.zeros((NX, NY), F32), unroll=True))

    for copy in strip_copies + cond_copies[:4]:
        copy.wait_recv()
    col0 = (lane24 & 3) == 0

    def face(outer, inner, turn_outer, turn_inner):
        vo, vi, co, ci = K[0, outer, 0:NX], K[0, inner, 0:NX], K[1, outer, 0:NX], K[1, inner, 0:NX]
        if turn_outer:
            vo, co = lanes(vo, turn_outer), lanes(co, turn_outer)
        if turn_inner:
            vi, ci = lanes(vi, turn_inner), lanes(ci, turn_inner)
        flux = jnp.where(col0, 0.5 * (co + ci) * (vo - vi), 0.0)
        for s in (4, 8, 16):
            flux = flux + lanes(flux, -s)
        return three_rows(flux) * (1.0 / COARSEN**3)

    rhs = tile_of(rsums)
    rhs = rhs + jnp.where((lane8 & 31) == 8, lanes(face(0, 1, -3, 0), 8), 0.0)
    rhs = rhs + jnp.where((lane8 & 31) == 23, lanes(face(5, 4, 0, -3), 23), 0.0)

    spot = lane8 & 31

    def widen(left, centre, right):
        out = jnp.where((spot >= 8) & (spot < 24), centre, 0.0)
        if left is not None:
            out = jnp.where((spot >= 4) & (spot < 8), lanes(left, -16), out)
            out = jnp.where((spot >= 24) & (spot < 28), lanes(right, 16), out)
        return out

    def stack(below, centre, above):
        top = jnp.where(row8 < 3, centre, jnp.where(row8 < 6, rows(above, 3), 0.0))
        bottom = jnp.where(row8 >= 5, rows(below, 5), 0.0)
        return jnp.concatenate([top, bottom], axis=0)

    def coarse_weights(c):
        c = c * (0.5 / COARSEN**2)
        ws = [c + lanes(c, 32), c + lanes(c, -32), c + rows(c, -1), c + rows(c, 1), c + lanes(c, -1), c + lanes(c, 1)]
        diag = SHIFT + (((ws[0] + ws[1]) + (ws[2] + ws[3])) + (ws[4] + ws[5]))
        inv = OMEGA / diag
        return inv, ws

    own = CS[...]
    inv, _ = coarse_weights(stack(CR[0], widen(CR[2], own, CR[3]), CR[1]))
    XS[...] = rhs * inv[0:8]
    start_copies = [send(XS, XR.at[i], xs.at[i], xr.at[i], d) for i, d in enumerate(NEIGHBOURS)]

    def image(z, d):
        up, dn = (z + 1) & (NZ - 1), (z + NZ - 1) & (NZ - 1)
        c = D[d, z]
        near = [D[d, up], D[d, dn], rows(c, -1), rows(c, 1), lanes(c, -1), lanes(c, 1)]
        terms = [W[i, z] * near[i] for i in range(6)]
        return c, ((terms[0] + terms[1]) + (terms[2] + terms[3])) + (terms[4] + terms[5])

    def sweep_one(z, carry):
        c, gain = image(z, 0)
        rt = (RT[z] - c) + gain
        RT[z] = rt
        D[1, z] = steps[0][0] * c + steps[0][1] * rt
        return carry

    def sweep_two(z, carry):
        c, gain = image(z, 1)
        rt = (RT[z] - c) + gain
        RT[z] = rt
        d = steps[1][0] * c + steps[1][1] * rt
        D[2, z] = d
        U[z] = D[0, z, 0:NX] + c[0:NX] + d[0:NX]
        return carry

    lax.fori_loop(0, NZ, sweep_one, 0, unroll=UNROLL)
    lax.fori_loop(0, NZ, sweep_two, 0, unroll=UNROLL)

    for copy in side_copies + diag_copies:
        copy.wait_recv()
    column = lane32 & 3
    ends, starts = column == 3, column == 0

    def strip_near(ref_of, g):
        x = ref_of(g)
        after, before = lanes(x, -1), lanes(x, 1)
        if g not in (2, 5):
            after = jnp.where(ends, lanes(ref_of(g + 1), 3), after)
        if g not in (0, 3):
            before = jnp.where(starts, lanes(ref_of(g - 1), -3), before)
        return x, [lanes(x, -4), lanes(x, 4), rows(x, -1), rows(x, 1), after, before]

    for g in range(6):
        c, cs_ = strip_near(lambda i: K[1, i], g)
        v, vs = strip_near(lambda i: K[0, i], g)
        ws = [c + n for n in cs_]
        total = ((ws[0] + ws[1]) + (ws[2] + ws[3])) + (ws[4] + ws[5])
        flow = ws[0] * vs[0]
        for i in range(1, 6):
            flow = flow + ws[i] * vs[i]
        diag = SHIFT + 0.5 * total
        inv = 1.0 / diag
        half = 0.5 * inv
        for i in range(6):
            KW[i, g] = ws[i] * half
        rt = ((K[2, g] - diag * v) + 0.5 * flow) * inv
        KR[g] = rt
        KD[0, g] = rt * (1.0 / theta)
    for k in range(SWEEPS):
        for g in range(6) if k < SWEEPS - 1 else (1, 4):
            c, near = strip_near(lambda i: KD[k, i], g)
            rt = KR[g] - c
            for i in range(6):
                rt = rt + KW[i, g] * near[i]
            KR[g] = rt
            KD[k + 1, g] = steps[k][0] * c + steps[k][1] * rt
    left = ((KD[0, 1] + KD[1, 1]) + (KD[2, 1] + KD[3, 1]))[0:NX]
    right = ((KD[0, 4] + KD[1, 4]) + (KD[2, 4] + KD[3, 4]))[0:NX]
    left = lanes(left, 4)
    even = (lane24 & 7) < 4
    EO[0] = jnp.where(even, right, left)
    EO[1] = jnp.where(even, left, right)

    for copy in cond_copies[4:] + start_copies:
        copy.wait_recv()

    def extended(ref, own):
        return stack(
            widen(ref[4], ref[0], ref[5]), widen(ref[2], own, ref[3]), widen(ref[6], ref[1], ref[7])
        )

    inv, ws = coarse_weights(extended(CR, own))
    ws = [w * inv for w in ws]
    start = extended(XR, XS[...])
    x = start
    for _ in range(COARSE_SWEEPS - 1):
        near = [lanes(x, 32), lanes(x, -32), rows(x, -1), rows(x, 1), lanes(x, -1), lanes(x, 1)]
        terms = [ws[i] * near[i] for i in range(6)]
        gain = ((terms[0] + terms[1]) + (terms[2] + terms[3])) + (terms[4] + terms[5])
        x = (start + (1.0 - OMEGA) * x) + gain
    x = x[0:8]
    for zc in range(NZC):
        spread = jnp.dot(x, ME[zc], precision=lax.Precision.HIGHEST, preferred_element_type=F32)
        for j in range(NXC):
            PR[zc, 8 * j : 8 * j + 8] = jnp.broadcast_to(spread[j : j + 1], (8, NY))

    edge = (lane24 < 4) | (lane24 >= NY - 4)

    def finish(z, carry):
        c, gain = image(z, 2)
        rt = (RT[z] - c) + gain
        d = steps[2][0] * c + steps[2][1] * rt
        total = U[z] + d[0:NX]
        strip = pltpu.roll(EO[z & 1], (2 * NY - 4 - 4 * z) & (NY - 1), 1)
        total = jnp.where(edge, strip, total)
        o_ref[z] = (V[z, 0:NX] + total) + PR[z // COARSEN]
        return carry

    lax.fori_loop(0, NZ, finish, 0, unroll=UNROLL)
    for copy in near_copies + side_copies + strip_copies + diag_copies + cond_copies + start_copies:
        copy.wait_send()


def solution(mesh):
    sizes = (mesh.shape["gx"], mesh.shape["gy"])

    def body(iterate, source, conduct):
        plane = (NZ, ROWS, NY)
        dma = pltpu.SemaphoreType.DMA
        return pl.pallas_call(
            functools.partial(kernel, sizes),
            out_shape=pltpu.VMEM((NZ, NX, NY), F32),
            in_specs=[pl.BlockSpec(memory_space=pl.ANY)] * 3,
            out_specs=pl.BlockSpec(memory_space=pltpu.VMEM),
            scratch_shapes=[
                pltpu.VMEM(plane, F32),
                pltpu.VMEM(plane, F32),
                pltpu.VMEM(plane, F32),
                pltpu.VMEM((6,) + plane, F32),
                pltpu.VMEM(plane, F32),
                pltpu.VMEM((3,) + plane, F32),
                pltpu.VMEM((NZ, NX, NY), F32),
                pltpu.VMEM((3, 6, ROWS, NY), F32),
                pltpu.VMEM((6, 6, ROWS, NY), F32),
                pltpu.VMEM((6, ROWS, NY), F32),
                pltpu.VMEM((4, 6, ROWS, NY), F32),
                pltpu.VMEM((2, NX, NY), F32),
                pltpu.VMEM((NZC, NX, NY), F32),
                pltpu.VMEM((NZC, NY, NY), F32),
                pltpu.VMEM((NZC, NY, NY), F32),
                pltpu.VMEM((8, NY), F32),
                pltpu.VMEM((8, 8, NY), F32),
                pltpu.VMEM((8, NY), F32),
                pltpu.VMEM((8, 8, NY), F32),
                dma((3,)),
                dma((6,)),
                dma((6,)),
                dma((8,)),
                dma((8,)),
                dma((8,)),
                dma((8,)),
                dma((8,)),
                dma((8,)),
            ],
            compiler_params=pltpu.CompilerParams(collective_id=0, has_side_effects=True),
        )(iterate, source, conduct)

    return jax.shard_map(
        body,
        mesh=mesh,
        in_specs=(P(None, "gx", "gy"), P(None, "gx", "gy"), P(None, "gx", "gy")),
        out_specs=P(None, "gx", "gy"),
        check_vma=False,
    )
```

```python
import functools

import jax
import jax.numpy as jnp
from jax import lax
from jax.experimental import pallas as pl
from jax.experimental.pallas import tpu as pltpu
from jax.sharding import PartitionSpec as P

SWEEPS = 3
COARSE_SWEEPS = 4
COARSEN = 8
SHIFT = 0.1
LMIN = 0.3
LMAX = 2.0
OMEGA = 0.8

MESH = pl.DeviceIdType.MESH
NZ, NX, NY = 32, 24, 128
RIM = 4
ROWS = NX + 2 * RIM
NZC, NXC, NYC = NZ // COARSEN, NX // COARSEN, NY // COARSEN
UNROLL = 8
F32 = jnp.float32
NEIGHBOURS = ((1, 0), (-1, 0), (0, 1), (0, -1), (1, 1), (1, -1), (-1, 1), (-1, -1))


def lanes(x, s):
    return pltpu.roll(x, s % x.shape[1], 1)


def rows(x, s):
    return pltpu.roll(x, s % x.shape[0], 0)


def iota(shape, dim):
    return lax.broadcasted_iota(jnp.int32, shape, dim)


def coefficients():
    theta = (LMAX + LMIN) / 2.0
    delta = (LMAX - LMIN) / 2.0
    sigma = theta / delta
    rho = 1.0 / sigma
    steps = []
    for _ in range(SWEEPS):
        after = 1.0 / (2.0 * sigma - rho)
        steps.append((after * rho, 2.0 * after / delta))
        rho = after
    return theta, steps


def kernel(sizes, v_hbm, s_hbm, c_hbm, o_ref, V, C, S, W, RT, D, U, K, KW, KR, KD, EO, MR, ME, CS, CR, XS, XR, TH, TO, PS,
           own_sem, ts, tr, fs, fr, ks, kr, cs, cr, xs, xr):
    ngx, ngy = sizes
    gx, gy = lax.axis_index("gx"), lax.axis_index("gy")

    def at(d):
        return (lax.rem(gx + d[0] + ngx, ngx), lax.rem(gy + d[1] + ngy, ngy))

    barrier = pltpu.get_barrier_semaphore()
    for d in NEIGHBOURS:
        pl.semaphore_signal(barrier, inc=1, device_id=at(d), device_id_type=MESH)
    loads = []
    for i, (src, dst) in enumerate(((v_hbm, V), (c_hbm, C), (s_hbm, S))):
        loads.append(pltpu.make_async_copy(src, dst.at[:, 0:NX, :], own_sem.at[i]))
        loads[-1].start()
    edges = []
    for i, src in enumerate((v_hbm, c_hbm)):
        edges.append(pltpu.make_async_copy(src.at[:, 0, :], TO.at[0, i], own_sem.at[3 + 2 * i]))
        edges.append(pltpu.make_async_copy(src.at[:, NX - 1, :], TO.at[1, i], own_sem.at[4 + 2 * i]))
    for copy in edges:
        copy.start()

    theta, steps = coefficients()
    lane24 = iota((NX, NY), 1)
    lane32 = iota((ROWS, NY), 1)
    lane8 = iota((8, NY), 1)
    row8 = iota((8, NY), 0)

    for zc in range(NZC):
        a, b = iota((NY, NY), 0), iota((NY, NY), 1)
        MR[zc] = jnp.where(b == zc * 32 + 8 + a // COARSEN, 1.0 / COARSEN**3, 0.0).astype(F32)
        ME[zc] = jnp.where(a == zc * 32 + 8 + b // COARSEN, 1.0, 0.0).astype(F32)

    def three_rows(x):
        out = jnp.zeros((8, NY), F32)
        for j in range(NXC):
            out = jnp.where(row8 == j, jnp.sum(x[8 * j : 8 * j + 8], axis=0, keepdims=True), out)
        return out

    def tile_of(sums):
        out = jnp.zeros((8, NY), F32)
        for zc in range(NZC):
            out = out + jnp.dot(sums[zc], MR[zc], precision=lax.Precision.HIGHEST, preferred_element_type=F32)
        return out

    def extract(f, ref):
        def step(m, accs):
            new = []
            for k in range(4):
                z = 4 * m + k
                turned = pltpu.roll(ref[z, 0:NX], 4 * z, 1)
                window = lax.shift_right_logical((lane24 + (8 - 4 * k + NY)) & (NY - 1), 4) == m
                new.append(jnp.where(window, turned, accs[k]))
            return tuple(new)

        accs = lax.fori_loop(0, 8, step, tuple(jnp.zeros((NX, NY), F32) for _ in range(4)), unroll=True)
        phase = lax.shift_right_logical(lane24, 2)

        def pick(j):
            out = accs[0]
            for k in range(1, 4):
                out = jnp.where(((phase + j) & 3) == k, accs[k], out)
            return out

        K[f, 1, 0:NX] = pick(0)
        K[f, 2, 0:NX] = lanes(pick(3), -4)
        K[f, 4, 0:NX] = lanes(pick(1), 4)
        K[f, 3, 0:NX] = lanes(pick(2), 8)

    for i, ref in enumerate((V, C, S)):
        loads[i].wait()
        extract(i, ref)
    csums = []
    for zc in range(NZC):
        csums.append(three_rows(functools.reduce(jnp.add, [C[zc * COARSEN + i, 0:NX] for i in range(COARSEN)])))
    CS[...] = tile_of(csums)

    row24 = iota((NX, NY), 0)
    inner = (row24 != NX - 1, row24 != 0, lane24 != NY - 1, lane24 != 0)

    def partial(z, acc):
        up, dn = (z + 1) & (NZ - 1), (z + NZ - 1) & (NZ - 1)
        c, v = C[z, 0:NX], V[z, 0:NX]
        total = (c + C[up, 0:NX]) * (V[up, 0:NX] - v) + (c + C[dn, 0:NX]) * (V[dn, 0:NX] - v)
        for turn, s, keep in zip((rows, rows, lanes, lanes), (-1, 1, -1, 1), inner):
            total = total + jnp.where(keep, (c + turn(c, s)) * (turn(v, s) - v), 0.0)
        return acc + ((S[z, 0:NX] - SHIFT * v) + 0.5 * total)

    for zc in range(NZC):
        PS[zc] = three_rows(
            lax.fori_loop(zc * COARSEN, (zc + 1) * COARSEN, partial, jnp.zeros((NX, NY), F32), unroll=True)
        )
    for copy in edges:
        copy.wait()

    pl.semaphore_wait(barrier, len(NEIGHBOURS))

    def send(src, dst, send_sem, recv_sem, d):
        copy = pltpu.make_async_remote_copy(
            src_ref=src, dst_ref=dst, send_sem=send_sem, recv_sem=recv_sem, device_id=at(d), device_id_type=MESH
        )
        copy.start()
        return copy

    low, high = slice(NX, NX + RIM), slice(NX + RIM, ROWS)
    first, last = slice(0, RIM), slice(NX - RIM, NX)
    thin_copies = []
    for i, src in enumerate((v_hbm, c_hbm)):
        thin_copies.append(send(src.at[:, NX - 1, :], TH.at[0, i], ts.at[2 * i], tr.at[2 * i], (1, 0)))
        thin_copies.append(send(src.at[:, 0, :], TH.at[1, i], ts.at[2 * i + 1], tr.at[2 * i + 1], (-1, 0)))
    strip_copies = [
        send(K.at[:, 4, 0:NX], K.at[:, 0, 0:NX], ks.at[2], kr.at[2], (0, 1)),
        send(K.at[:, 1, 0:NX], K.at[:, 5, 0:NX], ks.at[3], kr.at[3], (0, -1)),
    ]
    cond_copies = [send(CS, CR.at[i], cs.at[i], cr.at[i], d) for i, d in enumerate(NEIGHBOURS)]
    diag_copies = [
        send(K.at[:, 4, last], K.at[:, 0, high], ks.at[4], kr.at[4], (1, 1)),
        send(K.at[:, 1, last], K.at[:, 5, high], ks.at[5], kr.at[5], (1, -1)),
        send(K.at[:, 4, first], K.at[:, 0, low], ks.at[6], kr.at[6], (-1, 1)),
        send(K.at[:, 1, first], K.at[:, 5, low], ks.at[7], kr.at[7], (-1, -1)),
    ]
    near_copies = []
    for i, (src, dst) in enumerate(((v_hbm, V), (c_hbm, C), (s_hbm, S))):
        near_copies.append(send(src.at[:, last, :], dst.at[:, high, :], fs.at[2 * i], fr.at[2 * i], (1, 0)))
        near_copies.append(send(src.at[:, first, :], dst.at[:, low, :], fs.at[2 * i + 1], fr.at[2 * i + 1], (-1, 0)))
    side_copies = [
        send(K.at[:, 1:5, last], K.at[:, 1:5, high], ks.at[0], kr.at[0], (1, 0)),
        send(K.at[:, 1:5, first], K.at[:, 1:5, low], ks.at[1], kr.at[1], (-1, 0)),
    ]


    for copy in thin_copies + strip_copies + cond_copies[:4]:
        copy.wait_recv()
    col0 = (lane24 & 3) == 0

    def face(outer, inner, turn_outer, turn_inner):
        vo, vi, co, ci = K[0, outer, 0:NX], K[0, inner, 0:NX], K[1, outer, 0:NX], K[1, inner, 0:NX]
        if turn_outer:
            vo, co = lanes(vo, turn_outer), lanes(co, turn_outer)
        if turn_inner:
            vi, ci = lanes(vi, turn_inner), lanes(ci, turn_inner)
        flux = jnp.where(col0, 0.5 * (co + ci) * (vo - vi), 0.0)
        for s in (4, 8, 16):
            flux = flux + lanes(flux, -s)
        return three_rows(flux) * (1.0 / COARSEN**3)

    def flux_rows(side, row):
        flux = 0.5 * (TO[side, 1] + TH[side, 1]) * (TH[side, 0] - TO[side, 0])
        return [
            jnp.where(row8 == row, jnp.sum(flux[8 * zc : 8 * zc + 8], axis=0, keepdims=True), 0.0) for zc in range(NZC)
        ]

    below, above = flux_rows(0, 0), flux_rows(1, NXC - 1)
    rhs = tile_of([PS[zc] + (below[zc] + above[zc]) for zc in range(NZC)])
    rhs = rhs + jnp.where((lane8 & 31) == 8, lanes(face(0, 1, -3, 0), 8), 0.0)
    rhs = rhs + jnp.where((lane8 & 31) == 23, lanes(face(5, 4, 0, -3), 23), 0.0)

    spot = lane8 & 31

    def widen(left, centre, right):
        out = jnp.where((spot >= 8) & (spot < 24), centre, 0.0)
        if left is not None:
            out = jnp.where((spot >= 4) & (spot < 8), lanes(left, -16), out)
            out = jnp.where((spot >= 24) & (spot < 28), lanes(right, 16), out)
        return out

    def stack(below, centre, above):
        top = jnp.where(row8 < 3, centre, jnp.where(row8 < 6, rows(above, 3), 0.0))
        bottom = jnp.where(row8 >= 5, rows(below, 5), 0.0)
        return jnp.concatenate([top, bottom], axis=0)

    def coarse_weights(c):
        c = c * (0.5 / COARSEN**2)
        ws = [c + lanes(c, 32), c + lanes(c, -32), c + rows(c, -1), c + rows(c, 1), c + lanes(c, -1), c + lanes(c, 1)]
        diag = SHIFT + (((ws[0] + ws[1]) + (ws[2] + ws[3])) + (ws[4] + ws[5]))
        inv = OMEGA / diag
        return inv, ws

    own = CS[...]
    inv, _ = coarse_weights(stack(CR[0], widen(CR[2], own, CR[3]), CR[1]))
    XS[...] = rhs * inv[0:8]
    start_copies = [send(XS, XR.at[i], xs.at[i], xr.at[i], d) for i, d in enumerate(NEIGHBOURS)]

    for copy in near_copies:
        copy.wait_recv()

    def setup(z, carry):
        up, dn = (z + 1) & (NZ - 1), (z + NZ - 1) & (NZ - 1)
        c, v = C[z], V[z]
        ws = [
            c + C[up],
            c + C[dn],
            c + rows(c, -1),
            c + rows(c, 1),
            c + lanes(c, -1),
            c + lanes(c, 1),
        ]
        vs = [V[up], V[dn], rows(v, -1), rows(v, 1), lanes(v, -1), lanes(v, 1)]
        total = ((ws[0] + ws[1]) + (ws[2] + ws[3])) + (ws[4] + ws[5])
        flow = ((ws[0] * vs[0] + ws[1] * vs[1]) + (ws[2] * vs[2] + ws[3] * vs[3])) + (ws[4] * vs[4] + ws[5] * vs[5])
        diag = SHIFT + 0.5 * total
        residual = (S[z] - diag * v) + 0.5 * flow
        inv = 1.0 / diag
        half = 0.5 * inv
        for i in range(6):
            W[i, z] = ws[i] * half
        rt = residual * inv
        RT[z] = rt
        D[0, z] = rt * (1.0 / theta)
        return carry

    lax.fori_loop(0, NZ, setup, 0, unroll=UNROLL)

    def image(z, d):
        up, dn = (z + 1) & (NZ - 1), (z + NZ - 1) & (NZ - 1)
        c = D[d, z]
        near = [D[d, up], D[d, dn], rows(c, -1), rows(c, 1), lanes(c, -1), lanes(c, 1)]
        terms = [W[i, z] * near[i] for i in range(6)]
        return c, ((terms[0] + terms[1]) + (terms[2] + terms[3])) + (terms[4] + terms[5])

    def sweep_one(z, carry):
        c, gain = image(z, 0)
        rt = (RT[z] - c) + gain
        RT[z] = rt
        D[1, z] = steps[0][0] * c + steps[0][1] * rt
        return carry

    def sweep_two(z, carry):
        c, gain = image(z, 1)
        rt = (RT[z] - c) + gain
        RT[z] = rt
        d = steps[1][0] * c + steps[1][1] * rt
        D[2, z] = d
        U[z] = D[0, z, 0:NX] + c[0:NX] + d[0:NX]
        return carry

    lax.fori_loop(0, NZ, sweep_one, 0, unroll=UNROLL)
    lax.fori_loop(0, NZ, sweep_two, 0, unroll=UNROLL)

    for copy in side_copies + diag_copies:
        copy.wait_recv()
    column = lane32 & 3
    ends, starts = column == 3, column == 0

    def strip_near(ref_of, g):
        x = ref_of(g)
        after, before = lanes(x, -1), lanes(x, 1)
        if g not in (2, 5):
            after = jnp.where(ends, lanes(ref_of(g + 1), 3), after)
        if g not in (0, 3):
            before = jnp.where(starts, lanes(ref_of(g - 1), -3), before)
        return x, [lanes(x, -4), lanes(x, 4), rows(x, -1), rows(x, 1), after, before]

    for g in range(6):
        c, cs_ = strip_near(lambda i: K[1, i], g)
        v, vs = strip_near(lambda i: K[0, i], g)
        ws = [c + n for n in cs_]
        total = ((ws[0] + ws[1]) + (ws[2] + ws[3])) + (ws[4] + ws[5])
        flow = ws[0] * vs[0]
        for i in range(1, 6):
            flow = flow + ws[i] * vs[i]
        diag = SHIFT + 0.5 * total
        inv = 1.0 / diag
        half = 0.5 * inv
        for i in range(6):
            KW[i, g] = ws[i] * half
        rt = ((K[2, g] - diag * v) + 0.5 * flow) * inv
        KR[g] = rt
        KD[0, g] = rt * (1.0 / theta)
    for k in range(SWEEPS):
        for g in range(6) if k < SWEEPS - 1 else (1, 4):
            c, near = strip_near(lambda i: KD[k, i], g)
            rt = KR[g] - c
            for i in range(6):
                rt = rt + KW[i, g] * near[i]
            KR[g] = rt
            KD[k + 1, g] = steps[k][0] * c + steps[k][1] * rt
    left = ((KD[0, 1] + KD[1, 1]) + (KD[2, 1] + KD[3, 1]))[0:NX]
    right = ((KD[0, 4] + KD[1, 4]) + (KD[2, 4] + KD[3, 4]))[0:NX]
    left = lanes(left, 4)
    even = (lane24 & 7) < 4
    EO[0] = jnp.where(even, right, left)
    EO[1] = jnp.where(even, left, right)

    edge = (lane24 < 4) | (lane24 >= NY - 4)

    def finish(z, carry):
        c, gain = image(z, 2)
        rt = (RT[z] - c) + gain
        d = steps[2][0] * c + steps[2][1] * rt
        total = U[z] + d[0:NX]
        strip = pltpu.roll(EO[z & 1], (2 * NY - 4 - 4 * z) & (NY - 1), 1)
        total = jnp.where(edge, strip, total)
        U[z] = V[z, 0:NX] + total
        return carry

    lax.fori_loop(0, NZ, finish, 0, unroll=UNROLL)
    for copy in cond_copies[4:]:
        copy.wait_recv()

    def extended(ref, own):
        return stack(
            widen(ref[4], ref[0], ref[5]), widen(ref[2], own, ref[3]), widen(ref[6], ref[1], ref[7])
        )

    inv, ws = coarse_weights(extended(CR, own))
    ws = [w * inv for w in ws]
    for copy in start_copies:
        copy.wait_recv()
    start = extended(XR, XS[...])
    x = start
    for _ in range(COARSE_SWEEPS - 1):
        near = [lanes(x, 32), lanes(x, -32), rows(x, -1), rows(x, 1), lanes(x, -1), lanes(x, 1)]
        terms = [ws[i] * near[i] for i in range(6)]
        gain = ((terms[0] + terms[1]) + (terms[2] + terms[3])) + (terms[4] + terms[5])
        x = (start + (1.0 - OMEGA) * x) + gain
    x = x[0:8]
    for zc in range(NZC):
        spread = jnp.dot(x, ME[zc], precision=lax.Precision.HIGHEST, preferred_element_type=F32)
        wide = [jnp.broadcast_to(spread[j : j + 1], (8, NY)) for j in range(NXC)]
        for z in range(zc * COARSEN, (zc + 1) * COARSEN):
            for j in range(NXC):
                o_ref[z, 8 * j : 8 * j + 8] = U[z, 8 * j : 8 * j + 8] + wide[j]

    for copy in thin_copies + near_copies + side_copies + strip_copies + diag_copies + cond_copies + start_copies:
        copy.wait_send()


def solution(mesh):
    sizes = (mesh.shape["gx"], mesh.shape["gy"])

    def body(iterate, source, conduct):
        plane = (NZ, ROWS, NY)
        dma = pltpu.SemaphoreType.DMA
        return pl.pallas_call(
            functools.partial(kernel, sizes),
            out_shape=pltpu.VMEM((NZ, NX, NY), F32),
            in_specs=[pl.BlockSpec(memory_space=pl.ANY)] * 3,
            out_specs=pl.BlockSpec(memory_space=pltpu.VMEM),
            scratch_shapes=[
                pltpu.VMEM(plane, F32),
                pltpu.VMEM(plane, F32),
                pltpu.VMEM(plane, F32),
                pltpu.VMEM((6,) + plane, F32),
                pltpu.VMEM(plane, F32),
                pltpu.VMEM((3,) + plane, F32),
                pltpu.VMEM((NZ, NX, NY), F32),
                pltpu.VMEM((3, 6, ROWS, NY), F32),
                pltpu.VMEM((6, 6, ROWS, NY), F32),
                pltpu.VMEM((6, ROWS, NY), F32),
                pltpu.VMEM((4, 6, ROWS, NY), F32),
                pltpu.VMEM((2, NX, NY), F32),
                pltpu.VMEM((NZC, NY, NY), F32),
                pltpu.VMEM((NZC, NY, NY), F32),
                pltpu.VMEM((8, NY), F32),
                pltpu.VMEM((8, 8, NY), F32),
                pltpu.VMEM((8, NY), F32),
                pltpu.VMEM((8, 8, NY), F32),
                pltpu.VMEM((2, 2, NZ, NY), F32),
                pltpu.VMEM((2, 2, NZ, NY), F32),
                pltpu.VMEM((NZC, 8, NY), F32),
                dma((7,)),
                dma((4,)),
                dma((4,)),
                dma((6,)),
                dma((6,)),
                dma((8,)),
                dma((8,)),
                dma((8,)),
                dma((8,)),
                dma((8,)),
                dma((8,)),
            ],
            compiler_params=pltpu.CompilerParams(collective_id=0, has_side_effects=True),
        )(iterate, source, conduct)

    return jax.shard_map(
        body,
        mesh=mesh,
        in_specs=(P(None, "gx", "gy"), P(None, "gx", "gy"), P(None, "gx", "gy")),
        out_specs=P(None, "gx", "gy"),
        check_vma=False,
    )
```

```python
import functools

import jax
import jax.numpy as jnp
from jax import lax
from jax.experimental import pallas as pl
from jax.experimental.pallas import tpu as pltpu
from jax.sharding import PartitionSpec as P

SWEEPS = 3
COARSE_SWEEPS = 4
COARSEN = 8
SHIFT = 0.1
LMIN = 0.3
LMAX = 2.0
OMEGA = 0.8

MESH = pl.DeviceIdType.MESH
NZ, NX, NY = 32, 24, 128
RIM = 4
ROWS = NX + 2 * RIM
NZC, NXC, NYC = NZ // COARSEN, NX // COARSEN, NY // COARSEN
UNROLL = 8
F32 = jnp.float32
NEIGHBOURS = ((1, 0), (-1, 0), (0, 1), (0, -1), (1, 1), (1, -1), (-1, 1), (-1, -1))


def lanes(x, s):
    return pltpu.roll(x, s % x.shape[1], 1)


def rows(x, s):
    return pltpu.roll(x, s % x.shape[0], 0)


def iota(shape, dim):
    return lax.broadcasted_iota(jnp.int32, shape, dim)


def coefficients():
    theta = (LMAX + LMIN) / 2.0
    delta = (LMAX - LMIN) / 2.0
    sigma = theta / delta
    rho = 1.0 / sigma
    steps = []
    for _ in range(SWEEPS):
        after = 1.0 / (2.0 * sigma - rho)
        steps.append((after * rho, 2.0 * after / delta))
        rho = after
    return theta, steps


def kernel(sizes, v_hbm, s_hbm, c_hbm, o_ref, V, C, S, W, RT, D, U, K, KW, KR, KD, EO, MR, ME, CS, CR, XS, XR, TH, TO, PT, KX, PX, AC, AX, FB, FX, XB,
           own_sem, go, ls, lr, ts, tr, fs, fr, ks, kr, cs, cr, xs, xr):
    ngx, ngy = sizes
    gx, gy = lax.axis_index("gx"), lax.axis_index("gy")

    def at(d):
        return (lax.rem(gx + d[0] + ngx, ngx), lax.rem(gy + d[1] + ngy, ngy))

    barrier = pltpu.get_barrier_semaphore()
    is_last, is_first = gx == ngx - 1, gx == 0
    for d in NEIGHBOURS:

        def greet(d=d):
            pl.semaphore_signal(barrier, inc=1, device_id=at(d), device_id_type=MESH)

        if d[0] == 1:
            pl.when(gx < ngx - 2)(greet)
        elif d[0] == 0:
            pl.when(gx != ngx - 1)(greet)
        else:
            greet()
    loads = []
    for i, (src, dst) in enumerate(((v_hbm, V), (c_hbm, C), (s_hbm, S))):
        loads.append(pltpu.make_async_copy(src, dst.at[:, 0:NX, :], own_sem.at[i]))
        loads[-1].start()
    edges = []
    for i, src in enumerate((v_hbm, c_hbm)):
        edges.append(pltpu.make_async_copy(src.at[:, 0, :], TO.at[0, i], own_sem.at[3 + 2 * i]))
        edges.append(pltpu.make_async_copy(src.at[:, NX - 1, :], TO.at[1, i], own_sem.at[4 + 2 * i]))
    for copy in edges:
        copy.start()

    def remote(src, dst, send_sem, recv_sem, d):
        return pltpu.make_async_remote_copy(
            src_ref=src, dst_ref=dst, send_sem=send_sem, recv_sem=recv_sem, device_id=at(d), device_id_type=MESH
        )

    low, high = slice(NX, NX + RIM), slice(NX + RIM, ROWS)
    first, last = slice(0, RIM), slice(NX - RIM, NX)
    thin_copies = []
    for i, src in enumerate((v_hbm, c_hbm)):
        thin_copies.append(remote(src.at[:, NX - 1, :], TH.at[0, i], ts.at[2 * i], tr.at[2 * i], (1, 0)))
        thin_copies.append(remote(src.at[:, 0, :], TH.at[1, i], ts.at[2 * i + 1], tr.at[2 * i + 1], (-1, 0)))
    strip_copies = [
        remote(K.at[:, 4, 0:NX], K.at[:, 0, 0:NX], ks.at[2], kr.at[2], (0, 1)),
        remote(K.at[:, 1, 0:NX], K.at[:, 5, 0:NX], ks.at[3], kr.at[3], (0, -1)),
    ]
    cond_copies = [remote(CS, CR.at[i], cs.at[i], cr.at[i], d) for i, d in enumerate(NEIGHBOURS)]
    diag_copies = [
        remote(K.at[:, 4, last], K.at[:, 0, high], ks.at[4], kr.at[4], (1, 1)),
        remote(K.at[:, 1, last], K.at[:, 5, high], ks.at[5], kr.at[5], (1, -1)),
        remote(K.at[:, 4, first], K.at[:, 0, low], ks.at[6], kr.at[6], (-1, 1)),
        remote(K.at[:, 1, first], K.at[:, 5, low], ks.at[7], kr.at[7], (-1, -1)),
    ]
    near_copies = []
    for i, (src, dst) in enumerate(((v_hbm, V), (c_hbm, C), (s_hbm, S))):
        near_copies.append(remote(src.at[:, last, :], dst.at[:, high, :], fs.at[2 * i], fr.at[2 * i], (1, 0)))
        near_copies.append(remote(src.at[:, first, :], dst.at[:, low, :], fs.at[2 * i + 1], fr.at[2 * i + 1], (-1, 0)))
    side_copies = [
        remote(K.at[:, 1:5, last], K.at[:, 1:5, high], ks.at[0], kr.at[0], (1, 0)),
        remote(K.at[:, 1:5, first], K.at[:, 1:5, low], ks.at[1], kr.at[1], (-1, 0)),
    ]

    def start(copies):
        for copy in copies:
            copy.start()

    up_rows = thin_copies[0::2] + near_copies[0::2]
    up_local = diag_copies[0:2] + [cond_copies[0], cond_copies[4], cond_copies[5], side_copies[0]]

    @pl.when(is_last)
    def _():
        pl.semaphore_wait(barrier, 3)
        for d in ((1, 0), (1, 1), (1, -1)):
            pl.semaphore_signal(go, inc=1, device_id=at(d), device_id_type=MESH)
        start(up_rows)

    theta, steps = coefficients()
    lane24 = iota((NX, NY), 1)
    lane32 = iota((ROWS, NY), 1)
    lane8 = iota((8, NY), 1)
    row8 = iota((8, NY), 0)

    for zc in range(NZC):
        a, b = iota((NY, NY), 0), iota((NY, NY), 1)
        MR[zc] = jnp.where(b == zc * 32 + 8 + a // COARSEN, 1.0 / COARSEN**3, 0.0).astype(F32)
        ME[zc] = jnp.where(a == zc * 32 + 8 + b // COARSEN, 1.0, 0.0).astype(F32)

    def three_rows(x):
        out = jnp.zeros((8, NY), F32)
        for j in range(NXC):
            out = jnp.where(row8 == j, jnp.sum(x[8 * j : 8 * j + 8], axis=0, keepdims=True), out)
        return out

    def tile_of(sums):
        out = jnp.zeros((8, NY), F32)
        for zc in range(NZC):
            out = out + jnp.dot(sums[zc], MR[zc], precision=lax.Precision.HIGHEST, preferred_element_type=F32)
        return out

    def extract(f, ref):
        def step(m, accs):
            new = []
            for k in range(4):
                z = 4 * m + k
                turned = pltpu.roll(ref[z, 0:NX], 4 * z, 1)
                window = lax.shift_right_logical((lane24 + (8 - 4 * k + NY)) & (NY - 1), 4) == m
                new.append(jnp.where(window, turned, accs[k]))
            return tuple(new)

        accs = lax.fori_loop(0, 8, step, tuple(jnp.zeros((NX, NY), F32) for _ in range(4)), unroll=True)
        phase = lax.shift_right_logical(lane24, 2)

        def pick(j):
            out = accs[0]
            for k in range(1, 4):
                out = jnp.where(((phase + j) & 3) == k, accs[k], out)
            return out

        K[f, 1, 0:NX] = pick(0)
        K[f, 2, 0:NX] = lanes(pick(3), -4)
        K[f, 4, 0:NX] = lanes(pick(1), 4)
        K[f, 3, 0:NX] = lanes(pick(2), 8)

    for i, ref in enumerate((V, C, S)):
        loads[i].wait()
        extract(i, ref)
    csums = []
    for zc in range(NZC):
        csums.append(three_rows(functools.reduce(jnp.add, [C[zc * COARSEN + i, 0:NX] for i in range(COARSEN)])))
    CS[...] = tile_of(csums)

    @pl.when(is_last)
    def _():
        start(up_local)

    row24 = iota((NX, NY), 0)
    inner = (row24 != NX - 1, row24 != 0, lane24 != NY - 1, lane24 != 0)

    def partial(z, acc):
        up, dn = (z + 1) & (NZ - 1), (z + NZ - 1) & (NZ - 1)
        c, v = C[z, 0:NX], V[z, 0:NX]
        total = (c + C[up, 0:NX]) * (V[up, 0:NX] - v) + (c + C[dn, 0:NX]) * (V[dn, 0:NX] - v)
        for turn, s, keep in zip((rows, rows, lanes, lanes), (-1, 1, -1, 1), inner):
            total = total + jnp.where(keep, (c + turn(c, s)) * (turn(v, s) - v), 0.0)
        return acc + ((S[z, 0:NX] - SHIFT * v) + 0.5 * total)

    PT[...] = tile_of(
        [
            three_rows(
                lax.fori_loop(zc * COARSEN, (zc + 1) * COARSEN, partial, jnp.zeros((NX, NY), F32), unroll=True)
            )
            for zc in range(NZC)
        ]
    )
    strips_up = [
        remote(K.at[0:2, 1, 0:NX], KX.at[0], ls.at[0], lr.at[0], (1, 0)),
        remote(K.at[0:2, 4, 0:NX], KX.at[1], ls.at[1], lr.at[1], (1, 0)),
        remote(K.at[0:2, 4, 0:NX], KX.at[2], ls.at[2], lr.at[2], (1, 1)),
        remote(K.at[0:2, 1, 0:NX], KX.at[3], ls.at[3], lr.at[3], (1, -1)),
        remote(PT, PX.at[0], ls.at[4], lr.at[4], (1, 1)),
        remote(PT, PX.at[1], ls.at[5], lr.at[5], (1, -1)),
    ]
    tile_up = remote(AC, AX, ls.at[6], lr.at[6], (1, 0))
    face_sides = [remote(FB, FX.at[0], ls.at[7], lr.at[7], (0, 1)), remote(FB, FX.at[1], ls.at[8], lr.at[8], (0, -1))]

    @pl.when(is_last)
    def _():
        start(strips_up)

    for copy in edges:
        copy.wait()

    down = thin_copies[1::2] + [cond_copies[i] for i in (1, 6, 7)] + diag_copies[2:] + near_copies[1::2] + side_copies[1:]
    side = strip_copies + cond_copies[2:4]

    @pl.when(is_last)
    def _():
        pl.semaphore_wait(go, 1)
        start(side + down)

    @pl.when(is_first)
    def _():
        pl.semaphore_wait(barrier, 5)
        start(side + up_rows + up_local)

    @pl.when(jnp.logical_not(is_last | is_first))
    def _():
        pl.semaphore_wait(barrier, len(NEIGHBOURS))

        @pl.when(gx == ngx - 2)
        def _():
            pl.semaphore_signal(go, inc=1, device_id=at((1, 0)), device_id_type=MESH)

        start(thin_copies + strip_copies + cond_copies + diag_copies + near_copies + side_copies)


    def flux_tile(side, row):
        flux = 0.5 * (TO[side, 1] + TH[side, 1]) * (TH[side, 0] - TO[side, 0])
        return tile_of(
            [jnp.where(row8 == row, jnp.sum(flux[8 * zc : 8 * zc + 8], axis=0, keepdims=True), 0.0) for zc in range(NZC)]
        )

    def take_below():
        for copy in thin_copies[0::2] + cond_copies[:1]:
            copy.wait_recv()
        FB[...] = flux_tile(0, 0)

    @pl.when(is_last)
    def _():
        take_below()
        AC[0] = PT[...] + FB[...]
        AC[1] = CR[0]
        tile_up.start()

    for copy in thin_copies[1::2] + strip_copies + cond_copies[1:4]:
        copy.wait_recv()
    col0 = (lane24 & 3) == 0

    def face(vo, co, vi, ci, turn_outer, turn_inner):
        if turn_outer:
            vo, co = lanes(vo, turn_outer), lanes(co, turn_outer)
        if turn_inner:
            vi, ci = lanes(vi, turn_inner), lanes(ci, turn_inner)
        flux = jnp.where(col0, 0.5 * (co + ci) * (vo - vi), 0.0)
        for s in (4, 8, 16):
            flux = flux + lanes(flux, -s)
        return three_rows(flux) * (1.0 / COARSEN**3)

    own_strip = lambda g: (K[0, g, 0:NX], K[1, g, 0:NX])
    far_strip = lambda g: (KX[g, 0], KX[g, 1])
    at_left = lambda x: jnp.where((lane8 & 31) == 8, lanes(x, 8), 0.0)
    at_right = lambda x: jnp.where((lane8 & 31) == 23, lanes(x, 23), 0.0)
    rhs = PT[...] + flux_tile(1, NXC - 1)
    rhs = rhs + at_left(face(*own_strip(0), *own_strip(1), -3, 0))
    rhs = rhs + at_right(face(*own_strip(5), *own_strip(4), 0, -3))

    spot = lane8 & 31

    def widen(left, centre, right):
        out = jnp.where((spot >= 8) & (spot < 24), centre, 0.0)
        if left is not None:
            out = jnp.where((spot >= 4) & (spot < 8), lanes(left, -16), out)
            out = jnp.where((spot >= 24) & (spot < 28), lanes(right, 16), out)
        return out

    def stack(below, centre, above):
        top = jnp.where(row8 < 3, centre, jnp.where(row8 < 6, rows(above, 3), 0.0))
        bottom = jnp.where(row8 >= 5, rows(below, 5), 0.0)
        return jnp.concatenate([top, bottom], axis=0)

    def coarse_weights(c):
        c = c * (0.5 / COARSEN**2)
        ws = [c + lanes(c, 32), c + lanes(c, -32), c + rows(c, -1), c + rows(c, 1), c + lanes(c, -1), c + lanes(c, 1)]
        diag = SHIFT + (((ws[0] + ws[1]) + (ws[2] + ws[3])) + (ws[4] + ws[5]))
        inv = OMEGA / diag
        return inv, ws

    @pl.when(jnp.logical_not(is_last))
    def _():
        take_below()

    own = CS[...]
    inv, _ = coarse_weights(stack(CR[0], widen(CR[2], own, CR[3]), CR[1]))
    XS[...] = (rhs + FB[...]) * inv[0:8]
    start_copies = [remote(XS, XR.at[i], xs.at[i], xr.at[i], d) for i, d in enumerate(NEIGHBOURS)]
    start_up = [start_copies[i] for i in (0, 4, 5)]
    start_rest = [start_copies[i] for i in (1, 2, 3, 6, 7)]

    @pl.when(jnp.logical_not(is_last))
    def _():
        start(start_up)

    start(start_rest[1:3])

    @pl.when(is_first)
    def _():
        start(face_sides)
        pl.semaphore_wait(go, 3)
        start(down)

    start(start_rest[:1] + start_rest[3:])


    for copy in near_copies:
        copy.wait_recv()

    def setup(z, carry):
        up, dn = (z + 1) & (NZ - 1), (z + NZ - 1) & (NZ - 1)
        c, v = C[z], V[z]
        ws = [
            c + C[up],
            c + C[dn],
            c + rows(c, -1),
            c + rows(c, 1),
            c + lanes(c, -1),
            c + lanes(c, 1),
        ]
        vs = [V[up], V[dn], rows(v, -1), rows(v, 1), lanes(v, -1), lanes(v, 1)]
        total = ((ws[0] + ws[1]) + (ws[2] + ws[3])) + (ws[4] + ws[5])
        flow = ((ws[0] * vs[0] + ws[1] * vs[1]) + (ws[2] * vs[2] + ws[3] * vs[3])) + (ws[4] * vs[4] + ws[5] * vs[5])
        diag = SHIFT + 0.5 * total
        residual = (S[z] - diag * v) + 0.5 * flow
        inv = 1.0 / diag
        half = 0.5 * inv
        for i in range(6):
            W[i, z] = ws[i] * half
        rt = residual * inv
        RT[z] = rt
        D[0, z] = rt * (1.0 / theta)
        return carry

    lax.fori_loop(0, NZ, setup, 0, unroll=UNROLL)

    def image(z, d):
        up, dn = (z + 1) & (NZ - 1), (z + NZ - 1) & (NZ - 1)
        c = D[d, z]
        near = [D[d, up], D[d, dn], rows(c, -1), rows(c, 1), lanes(c, -1), lanes(c, 1)]
        terms = [W[i, z] * near[i] for i in range(6)]
        return c, ((terms[0] + terms[1]) + (terms[2] + terms[3])) + (terms[4] + terms[5])

    def sweep_one(z, carry):
        c, gain = image(z, 0)
        rt = (RT[z] - c) + gain
        RT[z] = rt
        D[1, z] = steps[0][0] * c + steps[0][1] * rt
        return carry

    def sweep_two(z, carry):
        c, gain = image(z, 1)
        rt = (RT[z] - c) + gain
        RT[z] = rt
        d = steps[1][0] * c + steps[1][1] * rt
        D[2, z] = d
        U[z] = D[0, z, 0:NX] + c[0:NX] + d[0:NX]
        return carry

    lax.fori_loop(0, NZ, sweep_one, 0, unroll=UNROLL)
    lax.fori_loop(0, NZ, sweep_two, 0, unroll=UNROLL)

    for copy in side_copies + diag_copies:
        copy.wait_recv()
    column = lane32 & 3
    ends, starts = column == 3, column == 0

    def strip_near(ref_of, g):
        x = ref_of(g)
        after, before = lanes(x, -1), lanes(x, 1)
        if g not in (2, 5):
            after = jnp.where(ends, lanes(ref_of(g + 1), 3), after)
        if g not in (0, 3):
            before = jnp.where(starts, lanes(ref_of(g - 1), -3), before)
        return x, [lanes(x, -4), lanes(x, 4), rows(x, -1), rows(x, 1), after, before]

    for g in range(6):
        c, cs_ = strip_near(lambda i: K[1, i], g)
        v, vs = strip_near(lambda i: K[0, i], g)
        ws = [c + n for n in cs_]
        total = ((ws[0] + ws[1]) + (ws[2] + ws[3])) + (ws[4] + ws[5])
        flow = ws[0] * vs[0]
        for i in range(1, 6):
            flow = flow + ws[i] * vs[i]
        diag = SHIFT + 0.5 * total
        inv = 1.0 / diag
        half = 0.5 * inv
        for i in range(6):
            KW[i, g] = ws[i] * half
        rt = ((K[2, g] - diag * v) + 0.5 * flow) * inv
        KR[g] = rt
        KD[0, g] = rt * (1.0 / theta)
    for k in range(SWEEPS):
        for g in range(6) if k < SWEEPS - 1 else (1, 4):
            c, near = strip_near(lambda i: KD[k, i], g)
            rt = KR[g] - c
            for i in range(6):
                rt = rt + KW[i, g] * near[i]
            KR[g] = rt
            KD[k + 1, g] = steps[k][0] * c + steps[k][1] * rt
    left = ((KD[0, 1] + KD[1, 1]) + (KD[2, 1] + KD[3, 1]))[0:NX]
    right = ((KD[0, 4] + KD[1, 4]) + (KD[2, 4] + KD[3, 4]))[0:NX]
    left = lanes(left, 4)
    even = (lane24 & 7) < 4
    EO[0] = jnp.where(even, right, left)
    EO[1] = jnp.where(even, left, right)

    edge = (lane24 < 4) | (lane24 >= NY - 4)

    def finish(z, carry):
        c, gain = image(z, 2)
        rt = (RT[z] - c) + gain
        d = steps[2][0] * c + steps[2][1] * rt
        total = U[z] + d[0:NX]
        strip = pltpu.roll(EO[z & 1], (2 * NY - 4 - 4 * z) & (NY - 1), 1)
        total = jnp.where(edge, strip, total)
        U[z] = V[z, 0:NX] + total
        return carry

    lax.fori_loop(0, NZ, finish, 0, unroll=UNROLL)
    for copy in cond_copies[4:]:
        copy.wait_recv()

    def bottom_of(x):
        return jnp.where(row8 >= 5, rows(x, 5), 0.0)

    def top_of(ref, own):
        above = widen(ref[6], ref[1], ref[7])
        return jnp.where(row8 < 3, widen(ref[2], own, ref[3]), jnp.where(row8 < 6, rows(above, 3), 0.0))

    cond_top, cond_bottom = top_of(CR, own), bottom_of(widen(CR[4], CR[0], CR[5]))
    inv, ws = coarse_weights(jnp.concatenate([cond_top, cond_bottom], axis=0))
    ws = [w * inv for w in ws]

    @pl.when(is_first)
    def _():
        for copy in strips_up + [tile_up] + face_sides:
            copy.wait_recv()
        further = jnp.where(row8 == 4, rows(widen(None, AX[1], None), 2), cond_bottom)
        inv, _ = coarse_weights(jnp.concatenate([cond_top, further], axis=0))
        left = face(*far_strip(2), *far_strip(0), -3, 0)
        right = face(*far_strip(3), *far_strip(1), 0, -3)
        centre = ((AX[0] + at_left(left)) + at_right(right)) - rows(FB[...], 2)
        before = (PX[0] - at_right(left)) - rows(FX[0], 2)
        after = (PX[1] - at_left(right)) - rows(FX[1], 2)
        XB[...] = bottom_of(widen(before, centre, after)) * inv[8:16]

    @pl.when(jnp.logical_not(is_first))
    def _():
        for copy in start_up:
            copy.wait_recv()
        XB[...] = bottom_of(widen(XR[4], XR[0], XR[5]))

    for copy in start_rest:
        copy.wait_recv()
    first_x = jnp.concatenate([top_of(XR, XS[...]), XB[...]], axis=0)
    x = first_x
    for _ in range(COARSE_SWEEPS - 1):
        near = [lanes(x, 32), lanes(x, -32), rows(x, -1), rows(x, 1), lanes(x, -1), lanes(x, 1)]
        terms = [ws[i] * near[i] for i in range(6)]
        gain = ((terms[0] + terms[1]) + (terms[2] + terms[3])) + (terms[4] + terms[5])
        x = (first_x + (1.0 - OMEGA) * x) + gain
    x = x[0:8]
    for zc in range(NZC):
        spread = jnp.dot(x, ME[zc], precision=lax.Precision.HIGHEST, preferred_element_type=F32)
        wide = [jnp.broadcast_to(spread[j : j + 1], (8, NY)) for j in range(NXC)]
        for z in range(zc * COARSEN, (zc + 1) * COARSEN):
            for j in range(NXC):
                o_ref[z, 8 * j : 8 * j + 8] = U[z, 8 * j : 8 * j + 8] + wide[j]

    for copy in thin_copies + near_copies + side_copies + strip_copies + diag_copies + cond_copies + start_rest:
        copy.wait_send()

    @pl.when(is_first)
    def _():
        for copy in face_sides:
            copy.wait_send()

    @pl.when(is_last)
    def _():
        for copy in strips_up + [tile_up]:
            copy.wait_send()

    @pl.when(jnp.logical_not(is_last))
    def _():
        for copy in start_up:
            copy.wait_send()


def solution(mesh):
    sizes = (mesh.shape["gx"], mesh.shape["gy"])

    def body(iterate, source, conduct):
        plane = (NZ, ROWS, NY)
        dma = pltpu.SemaphoreType.DMA
        return pl.pallas_call(
            functools.partial(kernel, sizes),
            out_shape=pltpu.VMEM((NZ, NX, NY), F32),
            in_specs=[pl.BlockSpec(memory_space=pl.ANY)] * 3,
            out_specs=pl.BlockSpec(memory_space=pltpu.VMEM),
            scratch_shapes=[
                pltpu.VMEM(plane, F32),
                pltpu.VMEM(plane, F32),
                pltpu.VMEM(plane, F32),
                pltpu.VMEM((6,) + plane, F32),
                pltpu.VMEM(plane, F32),
                pltpu.VMEM((3,) + plane, F32),
                pltpu.VMEM((NZ, NX, NY), F32),
                pltpu.VMEM((3, 6, ROWS, NY), F32),
                pltpu.VMEM((6, 6, ROWS, NY), F32),
                pltpu.VMEM((6, ROWS, NY), F32),
                pltpu.VMEM((4, 6, ROWS, NY), F32),
                pltpu.VMEM((2, NX, NY), F32),
                pltpu.VMEM((NZC, NY, NY), F32),
                pltpu.VMEM((NZC, NY, NY), F32),
                pltpu.VMEM((8, NY), F32),
                pltpu.VMEM((8, 8, NY), F32),
                pltpu.VMEM((8, NY), F32),
                pltpu.VMEM((8, 8, NY), F32),
                pltpu.VMEM((2, 2, NZ, NY), F32),
                pltpu.VMEM((2, 2, NZ, NY), F32),
                pltpu.VMEM((8, NY), F32),
                pltpu.VMEM((4, 2, NX, NY), F32),
                pltpu.VMEM((2, 8, NY), F32),
                pltpu.VMEM((2, 8, NY), F32),
                pltpu.VMEM((2, 8, NY), F32),
                pltpu.VMEM((8, NY), F32),
                pltpu.VMEM((2, 8, NY), F32),
                pltpu.VMEM((8, NY), F32),
                dma((7,)),
                pltpu.SemaphoreType.REGULAR,
                dma((9,)),
                dma((9,)),
                dma((4,)),
                dma((4,)),
                dma((6,)),
                dma((6,)),
                dma((8,)),
                dma((8,)),
                dma((8,)),
                dma((8,)),
                dma((8,)),
                dma((8,)),
            ],
            compiler_params=pltpu.CompilerParams(collective_id=0, has_side_effects=True),
        )(iterate, source, conduct)

    return jax.shard_map(
        body,
        mesh=mesh,
        in_specs=(P(None, "gx", "gy"), P(None, "gx", "gy"), P(None, "gx", "gy")),
        out_specs=P(None, "gx", "gy"),
        check_vma=False,
    )
```

```python
import functools

import jax
import jax.numpy as jnp
from jax import lax
from jax.experimental import pallas as pl
from jax.experimental.pallas import tpu as pltpu
from jax.sharding import PartitionSpec as P

SWEEPS = 3
COARSE_SWEEPS = 4
COARSEN = 8
SHIFT = 0.1
LMIN = 0.3
LMAX = 2.0
OMEGA = 0.8

MESH = pl.DeviceIdType.MESH
NZ, NX, NY = 32, 24, 128
RIM = 4
ROWS = NX + 2 * RIM
NZC, NXC, NYC = NZ // COARSEN, NX // COARSEN, NY // COARSEN
UNROLL = 8
F32 = jnp.float32
NEIGHBOURS = ((1, 0), (-1, 0), (0, 1), (0, -1), (1, 1), (1, -1), (-1, 1), (-1, -1))


def lanes(x, s):
    return pltpu.roll(x, s % x.shape[1], 1)


def rows(x, s):
    return pltpu.roll(x, s % x.shape[0], 0)


def iota(shape, dim):
    return lax.broadcasted_iota(jnp.int32, shape, dim)


def coefficients():
    theta = (LMAX + LMIN) / 2.0
    delta = (LMAX - LMIN) / 2.0
    sigma = theta / delta
    rho = 1.0 / sigma
    steps = []
    for _ in range(SWEEPS):
        after = 1.0 / (2.0 * sigma - rho)
        steps.append((after * rho, 2.0 * after / delta))
        rho = after
    return theta, steps


def kernel(sizes, v_hbm, s_hbm, c_hbm, U, PR, V, C, S, W, RT, D, K, KW, KR, KD, EO, MR, ME, CS, CR, XS, XR, TH, TO, PT, KX, PX, AC, AX, FB, FX, XB,
           own_sem, go, ls, lr, ts, tr, fs, fr, ks, kr, cs, cr, xs, xr):
    ngx, ngy = sizes
    gx, gy = lax.axis_index("gx"), lax.axis_index("gy")

    def at(d):
        return (lax.rem(gx + d[0] + ngx, ngx), lax.rem(gy + d[1] + ngy, ngy))

    barrier = pltpu.get_barrier_semaphore()
    is_last, is_first = gx == ngx - 1, gx == 0
    for d in NEIGHBOURS:

        def greet(d=d):
            pl.semaphore_signal(barrier, inc=1, device_id=at(d), device_id_type=MESH)

        if d[0] == 1:
            pl.when(gx < ngx - 2)(greet)
        elif d[0] == 0:
            pl.when(gx != ngx - 1)(greet)
        else:
            greet()
    loads = []
    for i, (src, dst) in enumerate(((c_hbm, C), (v_hbm, V), (s_hbm, S))):
        loads.append(pltpu.make_async_copy(src, dst.at[:, 0:NX, :], own_sem.at[i]))
        loads[-1].start()
    edges = []
    for i, src in enumerate((v_hbm, c_hbm)):
        edges.append(pltpu.make_async_copy(src.at[:, 0, :], TO.at[0, i], own_sem.at[3 + 2 * i]))
        edges.append(pltpu.make_async_copy(src.at[:, NX - 1, :], TO.at[1, i], own_sem.at[4 + 2 * i]))
    for copy in edges:
        copy.start()

    def remote(src, dst, send_sem, recv_sem, d):
        return pltpu.make_async_remote_copy(
            src_ref=src, dst_ref=dst, send_sem=send_sem, recv_sem=recv_sem, device_id=at(d), device_id_type=MESH
        )

    low, high = slice(NX, NX + RIM), slice(NX + RIM, ROWS)
    first, last = slice(0, RIM), slice(NX - RIM, NX)
    thin_copies = []
    for i, src in enumerate((v_hbm, c_hbm)):
        thin_copies.append(remote(src.at[:, NX - 1, :], TH.at[0, i], ts.at[2 * i], tr.at[2 * i], (1, 0)))
        thin_copies.append(remote(src.at[:, 0, :], TH.at[1, i], ts.at[2 * i + 1], tr.at[2 * i + 1], (-1, 0)))
    strip_copies = [
        remote(K.at[:, 4, 0:NX], K.at[:, 0, 0:NX], ks.at[2], kr.at[2], (0, 1)),
        remote(K.at[:, 1, 0:NX], K.at[:, 5, 0:NX], ks.at[3], kr.at[3], (0, -1)),
    ]
    cond_copies = [remote(CS, CR.at[i], cs.at[i], cr.at[i], d) for i, d in enumerate(NEIGHBOURS)]
    diag_copies = [
        remote(K.at[:, 4, last], K.at[:, 0, high], ks.at[4], kr.at[4], (1, 1)),
        remote(K.at[:, 1, last], K.at[:, 5, high], ks.at[5], kr.at[5], (1, -1)),
        remote(K.at[:, 4, first], K.at[:, 0, low], ks.at[6], kr.at[6], (-1, 1)),
        remote(K.at[:, 1, first], K.at[:, 5, low], ks.at[7], kr.at[7], (-1, -1)),
    ]
    near_copies = []
    for i, (src, dst, n) in enumerate(((v_hbm, V, RIM), (c_hbm, C, RIM), (s_hbm, S, RIM - 1))):
        upper, lower = (src.at[:, NX - n : NX, :], dst.at[:, ROWS - n : ROWS, :]), (src.at[:, 0:n, :], dst.at[:, NX : NX + n, :])
        near_copies.append(remote(*upper, fs.at[2 * i], fr.at[2 * i], (1, 0)))
        near_copies.append(remote(*lower, fs.at[2 * i + 1], fr.at[2 * i + 1], (-1, 0)))
    side_copies = [
        remote(K.at[:, 1:5, last], K.at[:, 1:5, high], ks.at[0], kr.at[0], (1, 0)),
        remote(K.at[:, 1:5, first], K.at[:, 1:5, low], ks.at[1], kr.at[1], (-1, 0)),
    ]

    def start(copies):
        for copy in copies:
            copy.start()

    up_thin, up_rows = thin_copies[0::2], near_copies[0::2]
    up_local = diag_copies[0:2] + side_copies[:1]

    @pl.when(is_last)
    def _():
        pl.semaphore_wait(barrier, 3)
        for d in ((1, 0), (1, 1), (1, -1)):
            pl.semaphore_signal(go, inc=1, device_id=at(d), device_id_type=MESH)
        start(up_thin)

    theta, steps = coefficients()
    lane24 = iota((NX, NY), 1)
    lane32 = iota((ROWS, NY), 1)
    lane8 = iota((8, NY), 1)
    row8 = iota((8, NY), 0)

    for zc in range(NZC):
        a, b = iota((NY, NY), 0), iota((NY, NY), 1)
        MR[zc] = jnp.where(b == zc * 32 + 8 + a // COARSEN, 1.0 / COARSEN**3, 0.0).astype(F32)
        ME[zc] = jnp.where(a == zc * 32 + 8 + b // COARSEN, 1.0, 0.0).astype(F32)

    def three_rows(x):
        out = jnp.zeros((8, NY), F32)
        for j in range(NXC):
            out = jnp.where(row8 == j, jnp.sum(x[8 * j : 8 * j + 8], axis=0, keepdims=True), out)
        return out

    def tile_of(sums):
        out = jnp.zeros((8, NY), F32)
        for zc in range(NZC):
            out = out + jnp.dot(sums[zc], MR[zc], precision=lax.Precision.HIGHEST, preferred_element_type=F32)
        return out

    def extract(f, ref):
        def step(m, accs):
            new = []
            for k in range(4):
                z = 4 * m + k
                turned = pltpu.roll(ref[z, 0:NX], 4 * z, 1)
                window = lax.shift_right_logical((lane24 + (8 - 4 * k + NY)) & (NY - 1), 4) == m
                new.append(jnp.where(window, turned, accs[k]))
            return tuple(new)

        accs = lax.fori_loop(0, 8, step, tuple(jnp.zeros((NX, NY), F32) for _ in range(4)), unroll=True)
        phase = lax.shift_right_logical(lane24, 2)

        def pick(j):
            out = accs[0]
            for k in range(1, 4):
                out = jnp.where(((phase + j) & 3) == k, accs[k], out)
            return out

        K[f, 1, 0:NX] = pick(0)
        K[f, 2, 0:NX] = lanes(pick(3), -4)
        K[f, 4, 0:NX] = lanes(pick(1), 4)
        K[f, 3, 0:NX] = lanes(pick(2), 8)

    loads[0].wait()
    csums = []
    for zc in range(NZC):
        csums.append(three_rows(functools.reduce(jnp.add, [C[zc * COARSEN + i, 0:NX] for i in range(COARSEN)])))
    CS[...] = tile_of(csums)

    @pl.when(is_last)
    def _():
        start([cond_copies[i] for i in (0, 4, 5)] + up_rows)

    for i, (f, ref) in enumerate(((1, C), (0, V), (2, S))):
        if i:
            loads[i].wait()
        extract(f, ref)

    @pl.when(is_last)
    def _():
        start(up_local)

    row24 = iota((NX, NY), 0)
    inner = (row24 != NX - 1, row24 != 0, lane24 != NY - 1, lane24 != 0)

    def partial(z, acc):
        up, dn = (z + 1) & (NZ - 1), (z + NZ - 1) & (NZ - 1)
        c, v = C[z, 0:NX], V[z, 0:NX]
        total = (c + C[up, 0:NX]) * (V[up, 0:NX] - v) + (c + C[dn, 0:NX]) * (V[dn, 0:NX] - v)
        for turn, s, keep in zip((rows, rows, lanes, lanes), (-1, 1, -1, 1), inner):
            total = total + jnp.where(keep, (c + turn(c, s)) * (turn(v, s) - v), 0.0)
        return acc + ((S[z, 0:NX] - SHIFT * v) + 0.5 * total)

    PT[...] = tile_of(
        [
            three_rows(
                lax.fori_loop(zc * COARSEN, (zc + 1) * COARSEN, partial, jnp.zeros((NX, NY), F32), unroll=True)
            )
            for zc in range(NZC)
        ]
    )
    strips_up = [
        remote(K.at[0:2, 1, 0:NX], KX.at[0], ls.at[0], lr.at[0], (1, 0)),
        remote(K.at[0:2, 4, 0:NX], KX.at[1], ls.at[1], lr.at[1], (1, 0)),
        remote(K.at[0:2, 4, 0:NX], KX.at[2], ls.at[2], lr.at[2], (1, 1)),
        remote(K.at[0:2, 1, 0:NX], KX.at[3], ls.at[3], lr.at[3], (1, -1)),
        remote(PT, PX.at[0], ls.at[4], lr.at[4], (1, 1)),
        remote(PT, PX.at[1], ls.at[5], lr.at[5], (1, -1)),
    ]
    tile_up = remote(AC, AX, ls.at[6], lr.at[6], (1, 0))
    face_sides = [remote(FB, FX.at[0], ls.at[7], lr.at[7], (0, 1)), remote(FB, FX.at[1], ls.at[8], lr.at[8], (0, -1))]

    @pl.when(is_last)
    def _():
        start(strips_up)

    for copy in edges:
        copy.wait()

    down = thin_copies[1::2] + [cond_copies[i] for i in (1, 6, 7)] + diag_copies[2:] + near_copies[1::2] + side_copies[1:]
    side = strip_copies + cond_copies[2:4]

    @pl.when(is_last)
    def _():
        pl.semaphore_wait(go, 1)
        start(side + down)

    @pl.when(is_first)
    def _():
        pl.semaphore_wait(barrier, 5)
        start(side + [cond_copies[i] for i in (0, 4, 5)] + up_thin + up_rows + up_local)

    @pl.when(jnp.logical_not(is_last | is_first))
    def _():
        pl.semaphore_wait(barrier, len(NEIGHBOURS))

        @pl.when(gx == ngx - 2)
        def _():
            pl.semaphore_signal(go, inc=1, device_id=at((1, 0)), device_id_type=MESH)

        start(thin_copies + strip_copies + cond_copies + diag_copies + near_copies + side_copies)


    def flux_tile(side, row):
        flux = 0.5 * (TO[side, 1] + TH[side, 1]) * (TH[side, 0] - TO[side, 0])
        return tile_of(
            [jnp.where(row8 == row, jnp.sum(flux[8 * zc : 8 * zc + 8], axis=0, keepdims=True), 0.0) for zc in range(NZC)]
        )

    def take_below():
        for copy in thin_copies[0::2] + cond_copies[:1]:
            copy.wait_recv()
        FB[...] = flux_tile(0, 0)

    @pl.when(is_last)
    def _():
        take_below()
        AC[0] = PT[...] + FB[...]
        AC[1] = CR[0]
        tile_up.start()

    for copy in thin_copies[1::2] + strip_copies + cond_copies[1:4]:
        copy.wait_recv()
    col0 = (lane24 & 3) == 0

    def face(vo, co, vi, ci, turn_outer, turn_inner):
        if turn_outer:
            vo, co = lanes(vo, turn_outer), lanes(co, turn_outer)
        if turn_inner:
            vi, ci = lanes(vi, turn_inner), lanes(ci, turn_inner)
        flux = jnp.where(col0, 0.5 * (co + ci) * (vo - vi), 0.0)
        for s in (4, 8, 16):
            flux = flux + lanes(flux, -s)
        return three_rows(flux) * (1.0 / COARSEN**3)

    own_strip = lambda g: (K[0, g, 0:NX], K[1, g, 0:NX])
    far_strip = lambda g: (KX[g, 0], KX[g, 1])
    at_left = lambda x: jnp.where((lane8 & 31) == 8, lanes(x, 8), 0.0)
    at_right = lambda x: jnp.where((lane8 & 31) == 23, lanes(x, 23), 0.0)
    rhs = PT[...] + flux_tile(1, NXC - 1)
    rhs = rhs + at_left(face(*own_strip(0), *own_strip(1), -3, 0))
    rhs = rhs + at_right(face(*own_strip(5), *own_strip(4), 0, -3))

    spot = lane8 & 31

    def widen(left, centre, right):
        out = jnp.where((spot >= 8) & (spot < 24), centre, 0.0)
        if left is not None:
            out = jnp.where((spot >= 4) & (spot < 8), lanes(left, -16), out)
            out = jnp.where((spot >= 24) & (spot < 28), lanes(right, 16), out)
        return out

    def stack(below, centre, above):
        top = jnp.where(row8 < 3, centre, jnp.where(row8 < 6, rows(above, 3), 0.0))
        bottom = jnp.where(row8 >= 5, rows(below, 5), 0.0)
        return jnp.concatenate([top, bottom], axis=0)

    def coarse_weights(c):
        c = c * (0.5 / COARSEN**2)
        ws = [c + lanes(c, 32), c + lanes(c, -32), c + rows(c, -1), c + rows(c, 1), c + lanes(c, -1), c + lanes(c, 1)]
        diag = SHIFT + (((ws[0] + ws[1]) + (ws[2] + ws[3])) + (ws[4] + ws[5]))
        inv = OMEGA / diag
        return inv, ws

    @pl.when(jnp.logical_not(is_last))
    def _():
        take_below()

    own = CS[...]
    inv, _ = coarse_weights(stack(CR[0], widen(CR[2], own, CR[3]), CR[1]))
    XS[...] = (rhs + FB[...]) * inv[0:8]
    start_copies = [remote(XS, XR.at[i], xs.at[i], xr.at[i], d) for i, d in enumerate(NEIGHBOURS)]
    start_up = [start_copies[i] for i in (0, 4, 5)]
    start_rest = [start_copies[i] for i in (1, 2, 3, 6, 7)]

    @pl.when(jnp.logical_not(is_last))
    def _():
        start(start_up)

    start(start_rest[1:3])

    @pl.when(is_first)
    def _():
        start(face_sides)
        pl.semaphore_wait(go, 3)
        start(down)

    start(start_rest[:1] + start_rest[3:])


    for copy in near_copies:
        copy.wait_recv()

    def setup(z, carry):
        up, dn = (z + 1) & (NZ - 1), (z + NZ - 1) & (NZ - 1)
        c, v = C[z], V[z]
        ws = [
            c + C[up],
            c + C[dn],
            c + rows(c, -1),
            c + rows(c, 1),
            c + lanes(c, -1),
            c + lanes(c, 1),
        ]
        vs = [V[up], V[dn], rows(v, -1), rows(v, 1), lanes(v, -1), lanes(v, 1)]
        total = ((ws[0] + ws[1]) + (ws[2] + ws[3])) + (ws[4] + ws[5])
        flow = ((ws[0] * vs[0] + ws[1] * vs[1]) + (ws[2] * vs[2] + ws[3] * vs[3])) + (ws[4] * vs[4] + ws[5] * vs[5])
        diag = SHIFT + 0.5 * total
        residual = (S[z] - diag * v) + 0.5 * flow
        inv = 1.0 / diag
        half = 0.5 * inv
        for i in range(6):
            W[i, z] = ws[i] * half
        rt = residual * inv
        RT[z] = rt
        D[0, z] = rt * (1.0 / theta)
        return carry

    lax.fori_loop(0, NZ, setup, 0, unroll=UNROLL)

    def image(z, d):
        up, dn = (z + 1) & (NZ - 1), (z + NZ - 1) & (NZ - 1)
        c = D[d, z]
        near = [D[d, up], D[d, dn], rows(c, -1), rows(c, 1), lanes(c, -1), lanes(c, 1)]
        terms = [W[i, z] * near[i] for i in range(6)]
        return c, ((terms[0] + terms[1]) + (terms[2] + terms[3])) + (terms[4] + terms[5])

    def sweep_one(z, carry):
        c, gain = image(z, 0)
        rt = (RT[z] - c) + gain
        RT[z] = rt
        D[1, z] = steps[0][0] * c + steps[0][1] * rt
        return carry

    def sweep_two(z, carry):
        c, gain = image(z, 1)
        rt = (RT[z] - c) + gain
        RT[z] = rt
        d = steps[1][0] * c + steps[1][1] * rt
        D[2, z] = d
        U[z] = D[0, z, 0:NX] + c[0:NX] + d[0:NX]
        return carry

    lax.fori_loop(0, NZ, sweep_one, 0, unroll=UNROLL)
    lax.fori_loop(0, NZ, sweep_two, 0, unroll=UNROLL)

    for copy in side_copies + diag_copies:
        copy.wait_recv()
    column = lane32 & 3
    ends, starts = column == 3, column == 0

    def strip_near(ref_of, g):
        x = ref_of(g)
        after, before = lanes(x, -1), lanes(x, 1)
        if g not in (2, 5):
            after = jnp.where(ends, lanes(ref_of(g + 1), 3), after)
        if g not in (0, 3):
            before = jnp.where(starts, lanes(ref_of(g - 1), -3), before)
        return x, [lanes(x, -4), lanes(x, 4), rows(x, -1), rows(x, 1), after, before]

    for g in range(6):
        c, cs_ = strip_near(lambda i: K[1, i], g)
        v, vs = strip_near(lambda i: K[0, i], g)
        ws = [c + n for n in cs_]
        total = ((ws[0] + ws[1]) + (ws[2] + ws[3])) + (ws[4] + ws[5])
        flow = ws[0] * vs[0]
        for i in range(1, 6):
            flow = flow + ws[i] * vs[i]
        diag = SHIFT + 0.5 * total
        inv = 1.0 / diag
        half = 0.5 * inv
        for i in range(6):
            KW[i, g] = ws[i] * half
        rt = ((K[2, g] - diag * v) + 0.5 * flow) * inv
        KR[g] = rt
        KD[0, g] = rt * (1.0 / theta)
    for k in range(SWEEPS):
        for g in range(6) if k < SWEEPS - 1 else (1, 4):
            c, near = strip_near(lambda i: KD[k, i], g)
            rt = KR[g] - c
            for i in range(6):
                rt = rt + KW[i, g] * near[i]
            KR[g] = rt
            KD[k + 1, g] = steps[k][0] * c + steps[k][1] * rt
    left = ((KD[0, 1] + KD[1, 1]) + (KD[2, 1] + KD[3, 1]))[0:NX]
    right = ((KD[0, 4] + KD[1, 4]) + (KD[2, 4] + KD[3, 4]))[0:NX]
    left = lanes(left, 4)
    even = (lane24 & 7) < 4
    EO[0] = jnp.where(even, right, left)
    EO[1] = jnp.where(even, left, right)

    edge = (lane24 < 4) | (lane24 >= NY - 4)

    def finish(z, carry):
        c, gain = image(z, 2)
        rt = (RT[z] - c) + gain
        d = steps[2][0] * c + steps[2][1] * rt
        total = U[z] + d[0:NX]
        strip = pltpu.roll(EO[z & 1], (2 * NY - 4 - 4 * z) & (NY - 1), 1)
        total = jnp.where(edge, strip, total)
        U[z] = V[z, 0:NX] + total
        return carry

    lax.fori_loop(0, NZ, finish, 0, unroll=UNROLL)
    for copy in cond_copies[4:]:
        copy.wait_recv()

    def bottom_of(x):
        return jnp.where(row8 >= 5, rows(x, 5), 0.0)

    def top_of(ref, own):
        above = widen(ref[6], ref[1], ref[7])
        return jnp.where(row8 < 3, widen(ref[2], own, ref[3]), jnp.where(row8 < 6, rows(above, 3), 0.0))

    cond_top, cond_bottom = top_of(CR, own), bottom_of(widen(CR[4], CR[0], CR[5]))
    inv, ws = coarse_weights(jnp.concatenate([cond_top, cond_bottom], axis=0))
    ws = [w * inv for w in ws]

    @pl.when(is_first)
    def _():
        for copy in strips_up + [tile_up] + face_sides:
            copy.wait_recv()
        further = jnp.where(row8 == 4, rows(widen(None, AX[1], None), 2), cond_bottom)
        inv, _ = coarse_weights(jnp.concatenate([cond_top, further], axis=0))
        left = face(*far_strip(2), *far_strip(0), -3, 0)
        right = face(*far_strip(3), *far_strip(1), 0, -3)
        centre = ((AX[0] + at_left(left)) + at_right(right)) - rows(FB[...], 2)
        before = (PX[0] - at_right(left)) - rows(FX[0], 2)
        after = (PX[1] - at_left(right)) - rows(FX[1], 2)
        XB[...] = bottom_of(widen(before, centre, after)) * inv[8:16]

    @pl.when(jnp.logical_not(is_first))
    def _():
        for copy in start_up:
            copy.wait_recv()
        XB[...] = bottom_of(widen(XR[4], XR[0], XR[5]))

    for copy in start_rest:
        copy.wait_recv()
    first_x = jnp.concatenate([top_of(XR, XS[...]), XB[...]], axis=0)
    x = first_x
    for _ in range(COARSE_SWEEPS - 1):
        near = [lanes(x, 32), lanes(x, -32), rows(x, -1), rows(x, 1), lanes(x, -1), lanes(x, 1)]
        terms = [ws[i] * near[i] for i in range(6)]
        gain = ((terms[0] + terms[1]) + (terms[2] + terms[3])) + (terms[4] + terms[5])
        x = (first_x + (1.0 - OMEGA) * x) + gain
    x = x[0:8]
    for zc in range(NZC):
        spread = jnp.dot(x, ME[zc], precision=lax.Precision.HIGHEST, preferred_element_type=F32)
        for j in range(NXC):
            PR[zc, 8 * j : 8 * j + 8] = jnp.broadcast_to(spread[j : j + 1], (8, NY))

    for copy in thin_copies + near_copies + side_copies + strip_copies + diag_copies + cond_copies + start_rest:
        copy.wait_send()

    @pl.when(is_first)
    def _():
        for copy in face_sides:
            copy.wait_send()

    @pl.when(is_last)
    def _():
        for copy in strips_up + [tile_up]:
            copy.wait_send()

    @pl.when(jnp.logical_not(is_last))
    def _():
        for copy in start_up:
            copy.wait_send()


def solution(mesh):
    sizes = (mesh.shape["gx"], mesh.shape["gy"])

    def body(iterate, source, conduct):
        plane = (NZ, ROWS, NY)
        dma = pltpu.SemaphoreType.DMA
        fine, coarse = pl.pallas_call(
            functools.partial(kernel, sizes),
            out_shape=(pltpu.VMEM((NZ, NX, NY), F32), pltpu.VMEM((NZC, NX, NY), F32)),
            in_specs=[pl.BlockSpec(memory_space=pl.ANY)] * 3,
            out_specs=(pl.BlockSpec(memory_space=pltpu.VMEM),) * 2,
            scratch_shapes=[
                pltpu.VMEM(plane, F32),
                pltpu.VMEM(plane, F32),
                pltpu.VMEM(plane, F32),
                pltpu.VMEM((6,) + plane, F32),
                pltpu.VMEM(plane, F32),
                pltpu.VMEM((3,) + plane, F32),
                pltpu.VMEM((3, 6, ROWS, NY), F32),
                pltpu.VMEM((6, 6, ROWS, NY), F32),
                pltpu.VMEM((6, ROWS, NY), F32),
                pltpu.VMEM((4, 6, ROWS, NY), F32),
                pltpu.VMEM((2, NX, NY), F32),
                pltpu.VMEM((NZC, NY, NY), F32),
                pltpu.VMEM((NZC, NY, NY), F32),
                pltpu.VMEM((8, NY), F32),
                pltpu.VMEM((8, 8, NY), F32),
                pltpu.VMEM((8, NY), F32),
                pltpu.VMEM((8, 8, NY), F32),
                pltpu.VMEM((2, 2, NZ, NY), F32),
                pltpu.VMEM((2, 2, NZ, NY), F32),
                pltpu.VMEM((8, NY), F32),
                pltpu.VMEM((4, 2, NX, NY), F32),
                pltpu.VMEM((2, 8, NY), F32),
                pltpu.VMEM((2, 8, NY), F32),
                pltpu.VMEM((2, 8, NY), F32),
                pltpu.VMEM((8, NY), F32),
                pltpu.VMEM((2, 8, NY), F32),
                pltpu.VMEM((8, NY), F32),
                dma((7,)),
                pltpu.SemaphoreType.REGULAR,
                dma((9,)),
                dma((9,)),
                dma((4,)),
                dma((4,)),
                dma((6,)),
                dma((6,)),
                dma((8,)),
                dma((8,)),
                dma((8,)),
                dma((8,)),
                dma((8,)),
                dma((8,)),
            ],
            compiler_params=pltpu.CompilerParams(collective_id=0, has_side_effects=True),
        )(iterate, source, conduct)
        fine = fine.reshape(NZC, COARSEN, NX, NY)
        return (fine + coarse[:, None]).reshape(NZ, NX, NY)

    return jax.shard_map(
        body,
        mesh=mesh,
        in_specs=(P(None, "gx", "gy"), P(None, "gx", "gy"), P(None, "gx", "gy")),
        out_specs=P(None, "gx", "gy"),
        check_vma=False,
    )
```
